256 devices in a mesh: branch: 2 (over core), dap: 32 (over y, z), crop: 4 (over x).
Axes of the slice: x: 4, y: 4, z: 8, core: 2. Of those that a mesh axis runs over, the one named last changes fastest.
Arguments:
- homolog_features: bfloat16 [2048, 256, 256], P(('crop', 'dap')), parts along dimension 0, may hold values from -6 to 6
- alignment_mask: int32 [2048, 256], P(('crop', 'dap')), parts along dimension 0, may hold values 0 or 1
- residue_mask: int32 [1024], P('crop'), parts along dimension 0, may hold values from 0 to 1, as said below
- pairwise_state: bfloat16 [1024, 256, 128], P(('crop', 'dap')), parts along dimension 0, may hold values from -6 to 6
- vertical_gain_vector: float32 [256], replicated, may hold values from 0.25 to 1.75
- fourfold_projection_matrix: bfloat16 [256, 4, 8, 32], P(None, None, 'branch'), may hold values from -0.375 to 0.375
- mixing_projection_matrix: bfloat16 [8, 32, 256], P('branch'), may hold values from -0.375 to 0.375
- product_gain_vector: float32 [256], replicated, may hold values from 0.25 to 1.75
- product_source_matrix: bfloat16 [256, 32], P(None, 'branch'), may hold values from -0.375 to 0.375
- product_target_matrix: bfloat16 [256, 32], replicated, may hold values from -0.375 to 0.375
- outer_output_weight: bfloat16 [32, 32, 128], P('branch'), may hold values from -4 to 4
- triangle_norm_scale: float32 [128], replicated, may hold values from 0.25 to 1.75
- triangle_input_weight: bfloat16 [128, 4, 128], P(None, None, 'branch'), may hold values from -0.5 to 0.5
- triangle_gate_weight: bfloat16 [128, 128], P(None, 'branch'), may hold values from -0.5 to 0.5
- hidden_norm_scale: float32 [128], P('branch'), may hold values from 0.25 to 1.75
- triangle_output_weight: bfloat16 [128, 128], P('branch'), may hold values from -0.5 to 0.5
Outputs:
- homolog_mixed: bfloat16 [2048, 256, 256], P('crop', 'dap'), parts along dimension 0
- pairwise_output: bfloat16 [1024, 256, 128], P(('crop', 'dap'), None, 'branch'), parts along dimension 0
The draws below stay inside these ranges and needn't reach their ends.
There are 4 independent parts, one for each index of `crop`. The reference program is written for one: setup_inputs(seed, part) draws one part's arguments, and reference() takes and returns one part's arrays. A program takes and returns all parts, laid end to end along the dimension named above; an argument that names none is the same for every part. Nothing has to cross between parts.
Inputs may be any that keep to these rules, and one draw needn't show every extreme that they name: residue_mask is 0 on a padded run at the crop's end of 1 to 65 residues, and 0 on some scattered unresolved residues before it; 1 elsewhere.
All inputs are finite; a program needn't handle non-finite values. No bound on the sum of `alignment_mask` on one device may be relied on, other than what follows from the above.
Results may differ from the reference program's by a relative error of at most 0.017.
Values may be sent and summed in bfloat16 or wider, within the bound.
A program may use at most 64 MiB of HBM per device.

```python
import jax
import jax.numpy as jnp
from jax import lax

HOMOLOG_DEPTH = 512
AMINO_SPAN = 256
FEATURE_DEPTH = 256
CZ = 128
PARALLEL_MAPS = 8
SUBSPACE_SIZE = 32
PRODUCT_FEATURES = 32
CH = 128


def draw_residue_mask(key, part):
    padding = jax.random.randint(jax.random.fold_in(key, 11), (), 1, AMINO_SPAN // 4 + 2)
    holes = jax.random.randint(jax.random.fold_in(key, 23), (AMINO_SPAN,), 0, 8)
    position = jnp.arange(AMINO_SPAN, dtype=jnp.int32)
    inside = (position < AMINO_SPAN - padding).astype(jnp.int32)
    resolved = (holes != 0).astype(jnp.int32)
    return inside * resolved


def touch_ends(entries, key, least, high):
    longest = entries.shape.index(max(entries.shape))
    spots = []
    for shift in (0, 1):
        where = [jax.random.randint(jax.random.fold_in(key, axis), (), 0, length) for axis, length in enumerate(entries.shape)]
        where[longest] = (where[longest] + shift) % entries.shape[longest]
        spots.append(tuple(where))
    return entries.at[spots[0]].set(least).at[spots[1]].set(high)


def level_of(stream_key, dims, pieces, low, high):
    gain, own = 1.0, jax.random.fold_in(stream_key, 6)
    for dim, blocks in pieces:
        steps = jnp.exp(jax.random.uniform(jax.random.fold_in(own, dim), (blocks,), jnp.float32, low / len(pieces), high / len(pieces)))
        gain = gain * jnp.repeat(steps, dims[dim] // blocks).reshape([-1 if axis == dim else 1 for axis in range(len(dims))])
    return gain


def scatter_about(key, shape, scale, limit, pieces=(), kind=jnp.bfloat16):
    result = scale * jax.random.normal(key, shape, jnp.float32)
    if pieces:
        result = result * level_of(key, shape, pieces, -0.22, 0.18)
    return jnp.clip(result, -limit, limit).astype(kind)


def setup_inputs(seed: int = 0, part: int = 0) -> dict:
    seeds = jax.random.split(jax.random.key(seed), 17)
    part_splits = jax.random.split(jax.random.fold_in(seeds[16], part), 17)
    return {
        "homolog_features": scatter_about(part_splits[0], (HOMOLOG_DEPTH, AMINO_SPAN, FEATURE_DEPTH), 1.0, 6.0, ((0, 32),)),
        "alignment_mask": touch_ends((jax.random.randint(part_splits[1], (HOMOLOG_DEPTH, AMINO_SPAN), 0, 5) < 4).astype(jnp.int32), jax.random.fold_in(part_splits[1], 1), 0, 1),
        "residue_mask": draw_residue_mask(jax.random.fold_in(jax.random.fold_in(seeds[16], part), 71), part),
        "pairwise_state": scatter_about(part_splits[3], (AMINO_SPAN, AMINO_SPAN, CZ), 1.0, 6.0, ((0, 32),)),
        "vertical_gain_vector": jnp.clip(1.0 + 0.15 * jax.random.normal(seeds[4], (FEATURE_DEPTH,), jnp.float32), 0.25, 1.75),
        "fourfold_projection_matrix": scatter_about(seeds[5], (FEATURE_DEPTH, 4, PARALLEL_MAPS, SUBSPACE_SIZE), FEATURE_DEPTH ** -0.5, 0.375, ((2, 2),)),
        "mixing_projection_matrix": scatter_about(seeds[6], (PARALLEL_MAPS, SUBSPACE_SIZE, FEATURE_DEPTH), (PARALLEL_MAPS * SUBSPACE_SIZE) ** -0.5, 0.375, ((0, 2),)),
        "product_gain_vector": jnp.clip(1.0 + 0.15 * jax.random.normal(seeds[7], (FEATURE_DEPTH,), jnp.float32), 0.25, 1.75),
        "product_source_matrix": scatter_about(seeds[8], (FEATURE_DEPTH, PRODUCT_FEATURES), FEATURE_DEPTH ** -0.5, 0.375, ((1, 2),)),
        "product_target_matrix": scatter_about(seeds[9], (FEATURE_DEPTH, PRODUCT_FEATURES), FEATURE_DEPTH ** -0.5, 0.375),
        "outer_output_weight": scatter_about(seeds[10], (PRODUCT_FEATURES, PRODUCT_FEATURES, CZ), 0.6, 4.0, ((0, 2),)),
        "triangle_norm_scale": jnp.clip(1.0 + 0.15 * jax.random.normal(seeds[11], (CZ,), jnp.float32), 0.25, 1.75),
        "triangle_input_weight": scatter_about(seeds[12], (CZ, 4, CH), CZ ** -0.5, 0.5, ((2, 2),)),
        "triangle_gate_weight": scatter_about(seeds[13], (CZ, CZ), CZ ** -0.5, 0.5, ((1, 2),)),
        "hidden_norm_scale": jnp.clip(1.0 + 0.15 * jax.random.normal(seeds[14], (CH,), jnp.float32), 0.25, 1.75),
        "triangle_output_weight": scatter_about(seeds[15], (CH, CZ), CH ** -0.5, 0.5, ((0, 2),)),
    }


eps_norm = 1e-05

def standardize_features(field, gain_vec):
    mean_val = lax.optimization_barrier(jnp.mean(field, axis=-1, keepdims=True))
    variance = lax.optimization_barrier(jnp.mean((field - mean_val) ** 2, axis=-1, keepdims=True))
    return (field - mean_val) * lax.rsqrt(variance + eps_norm) * gain_vec.astype(jnp.float32)

def reference(homolog_features, alignment_mask, residue_mask, pairwise_state, vertical_gain_vector, fourfold_projection_matrix, mixing_projection_matrix, product_gain_vector, product_source_matrix, product_target_matrix, outer_output_weight, triangle_norm_scale, triangle_input_weight, triangle_gate_weight, hidden_norm_scale, triangle_output_weight):
    residue_active = residue_mask.astype(jnp.float32)
    effective_mask = alignment_mask.astype(jnp.float32) * residue_active[None, :]
    entering_matrix = fourfold_projection_matrix.reshape(FEATURE_DEPTH, 4 * PARALLEL_MAPS * SUBSPACE_SIZE)
    leaving_matrix = mixing_projection_matrix.reshape(PARALLEL_MAPS * SUBSPACE_SIZE, FEATURE_DEPTH)
    inv_root = 1.0 / SUBSPACE_SIZE ** 0.5

    def single_column(operands):
        column_index, keep_mask = operands
        normalized_input = standardize_features(column_index.astype(jnp.float32), vertical_gain_vector).astype(jnp.bfloat16)
        projection = jnp.dot(normalized_input, entering_matrix, preferred_element_type=jnp.float32).reshape(HOMOLOG_DEPTH, 4, PARALLEL_MAPS, SUBSPACE_SIZE)
        queries = projection[:, 0].astype(jnp.bfloat16)
        key_vecs = projection[:, 1].astype(jnp.bfloat16)
        values = projection[:, 2].astype(jnp.bfloat16)
        gating = jax.nn.sigmoid(projection[:, 3])
        scores = jnp.einsum('shd,thd->hst', queries.astype(jnp.float32), key_vecs.astype(jnp.float32)) * inv_root
        scores = jnp.where((keep_mask > 0.5)[None, None, :], scores, -1000000000.0)
        weights = jax.nn.softmax(scores, axis=-1).astype(jnp.bfloat16)
        attended = jnp.einsum('hst,thd->shd', weights.astype(jnp.float32), values.astype(jnp.float32))
        gated_out = (attended * gating).astype(jnp.bfloat16).reshape(HOMOLOG_DEPTH, PARALLEL_MAPS * SUBSPACE_SIZE)
        return jnp.dot(gated_out, leaving_matrix, preferred_element_type=jnp.float32)
    head_contributions = lax.map(single_column, (jnp.moveaxis(homolog_features, 1, 0), effective_mask.T))
    homolog_mixed = (homolog_features.astype(jnp.float32) + jnp.moveaxis(head_contributions, 0, 1)).astype(jnp.bfloat16)
    product_standardized = standardize_features(homolog_mixed.astype(jnp.float32), product_gain_vector).astype(jnp.bfloat16).reshape(HOMOLOG_DEPTH * AMINO_SPAN, FEATURE_DEPTH)
    left_panel = (jnp.dot(product_standardized, product_source_matrix, preferred_element_type=jnp.float32).reshape(HOMOLOG_DEPTH, AMINO_SPAN, PRODUCT_FEATURES) * effective_mask[..., None]).astype(jnp.bfloat16)
    right_panel = (jnp.dot(product_standardized, product_target_matrix, preferred_element_type=jnp.float32).reshape(HOMOLOG_DEPTH, AMINO_SPAN, PRODUCT_FEATURES) * effective_mask[..., None]).astype(jnp.bfloat16)
    pair_counts = jnp.dot(effective_mask.T, effective_mask, precision=lax.Precision.HIGHEST)
    right_flat = right_panel.reshape(HOMOLOG_DEPTH, AMINO_SPAN * PRODUCT_FEATURES)
    out_flat = outer_output_weight.reshape(PRODUCT_FEATURES * PRODUCT_FEATURES, CZ)

    def opm_row(operands):
        left_row, count_row = operands
        outer_prod = jnp.dot(left_row.T, right_flat, preferred_element_type=jnp.float32)
        outer_prod = outer_prod.reshape(PRODUCT_FEATURES, AMINO_SPAN, PRODUCT_FEATURES).transpose(1, 0, 2).reshape(AMINO_SPAN, PRODUCT_FEATURES * PRODUCT_FEATURES).astype(jnp.bfloat16)
        update = jnp.dot(outer_prod, out_flat, preferred_element_type=jnp.float32)
        return update / jnp.maximum(count_row, 1.0)[:, None]
    update = lax.map(opm_row, (jnp.moveaxis(left_panel, 1, 0), pair_counts))
    pair_mid = (pairwise_state.astype(jnp.float32) + update).astype(jnp.bfloat16)
    pair_field = pair_mid.astype(jnp.float32)
    pair_normed = standardize_features(pair_field, triangle_norm_scale).astype(jnp.bfloat16).reshape(AMINO_SPAN * AMINO_SPAN, CZ)
    projection = jnp.dot(pair_normed, triangle_input_weight.reshape(CZ, 4 * CH), preferred_element_type=jnp.float32).reshape(AMINO_SPAN, AMINO_SPAN, 4, CH)
    pair_live = (residue_active[:, None] * residue_active[None, :])[..., None]
    tri_left = (pair_live * jax.nn.sigmoid(projection[:, :, 0]) * projection[:, :, 1]).astype(jnp.bfloat16)
    tri_right = (pair_live * jax.nn.sigmoid(projection[:, :, 2]) * projection[:, :, 3]).astype(jnp.bfloat16)
    tri_sum = jnp.einsum('cik,cjk->cij', jnp.moveaxis(tri_left, 2, 0).astype(jnp.float32), jnp.moveaxis(tri_right, 2, 0).astype(jnp.float32))
    mean_val = lax.optimization_barrier(jnp.mean(tri_sum, axis=0, keepdims=True))
    variance = lax.optimization_barrier(jnp.mean((tri_sum - mean_val) ** 2, axis=0, keepdims=True))
    tri_scaled = ((tri_sum - mean_val) * lax.rsqrt(variance + eps_norm) * hidden_norm_scale[:, None, None]).astype(jnp.bfloat16)
    projected = lax.dot_general(tri_scaled, triangle_output_weight, (((0,), (0,)), ((), ())), preferred_element_type=jnp.float32)
    gating = jax.nn.sigmoid(jnp.dot(pair_normed, triangle_gate_weight, preferred_element_type=jnp.float32)).reshape(AMINO_SPAN, AMINO_SPAN, CZ)
    pairwise_output = (pair_field + gating * projected).astype(jnp.bfloat16)
    return (homolog_mixed, pairwise_output)
```

```python
import functools

import jax
import jax.numpy as jnp
from jax import lax
from jax.experimental import pallas as pl
from jax.experimental.pallas import tpu as pltpu
from jax.sharding import PartitionSpec as P

eps_norm = 1e-05
SWAP = ((0, 1), (1, 0))
NT = (((1,), (1,)), ((), ()))
TN = (((0,), (0,)), ((), ()))


def standardize_features(field, gain_vec):
    mean_val = jnp.mean(field, axis=-1, keepdims=True)
    variance = jnp.mean((field - mean_val) ** 2, axis=-1, keepdims=True)
    return (field - mean_val) * lax.rsqrt(variance + eps_norm) * gain_vec


def sigmoid(x):
    return 1.0 / (1.0 + jnp.exp(-x))


def dot(a, b, dims):
    return lax.dot_general(a, b, dims, preferred_element_type=jnp.float32)


def column_kernel(
    heads, x_ref, mrow_ref, mcol_ref, gain_ref, w_ref, wo_ref, gain2_ref, wp_ref, mixed_ref, left_ref, right_ref,
    qkv_ref, gate_ref, gated_ref,
):
    width = x_ref.shape[-1]
    depth = mrow_ref.shape[-1]
    feats = wo_ref.shape[0]
    hd = feats // heads
    x = x_ref[:, 0].reshape(depth, width).astype(jnp.float32)
    n = standardize_features(x, gain_ref[...]).astype(jnp.bfloat16)
    proj = dot(w_ref[...], n, NT)
    for i in range(3):
        qkv_ref[i] = proj[i * feats : (i + 1) * feats].astype(jnp.bfloat16).reshape(heads, hd, depth)
    gate_ref[...] = sigmoid(proj[3 * feats :]).reshape(heads, hd, depth)
    live = mcol_ref[0] > 0.5
    inv_root = 1.0 / hd**0.5

    def one_head(h):
        scores = dot(qkv_ref[1, h], qkv_ref[0, h], TN) * inv_root
        scores = jnp.where(live, scores, -1000000000.0)
        e = jnp.exp(scores - jnp.max(scores, axis=0, keepdims=True))
        total = jnp.sum(e, axis=0, keepdims=True)
        att = jnp.dot(qkv_ref[2, h], e.astype(jnp.bfloat16), preferred_element_type=jnp.float32)
        gated_ref[h] = (att * (1.0 / total) * gate_ref[h]).astype(jnp.bfloat16)

    unroll = 4

    @pl.loop(0, heads // unroll)
    def _(step):
        for u in range(unroll):
            one_head(step * unroll + u)

    gated = gated_ref[...].reshape(feats, depth)
    mixed = (x + dot(gated, wo_ref[...], TN)).astype(jnp.bfloat16)
    mixed_ref[0] = mixed
    n2 = standardize_features(mixed.astype(jnp.float32), gain2_ref[...]).astype(jnp.bfloat16)
    panel = (dot(wp_ref[...], n2, NT) * mrow_ref[0]).astype(jnp.bfloat16)
    chans = left_ref.shape[1]
    left_ref[0] = panel[:chans]
    right_ref[0] = panel[chans:]


def column_stage(xs, mask_rows, gain, w_t, wo, gain2, wp_t, heads):
    groups, res, s_loc, width = xs.shape
    depth = groups * s_loc
    chans = wp_t.shape[0] // 2
    whole = lambda a: pl.BlockSpec(a.shape, lambda i: (0,) * a.ndim)
    mrow = mask_rows[:, None, :]
    mcol = mask_rows[:, :, None]
    return pl.pallas_call(
        functools.partial(column_kernel, heads),
        grid=(res,),
        in_specs=[
            pl.BlockSpec((groups, 1, s_loc, width), lambda i: (0, i, 0, 0)),
            pl.BlockSpec((1, 1, depth), lambda i: (i, 0, 0)),
            pl.BlockSpec((1, depth, 1), lambda i: (i, 0, 0)),
            whole(gain),
            whole(w_t),
            whole(wo),
            whole(gain2),
            whole(wp_t),
        ],
        out_specs=[
            pl.BlockSpec((1, depth, width), lambda i: (i, 0, 0)),
            pl.BlockSpec((1, chans, depth), lambda i: (i, 0, 0)),
            pl.BlockSpec((1, chans, depth), lambda i: (i, 0, 0)),
        ],
        out_shape=[
            jax.ShapeDtypeStruct((res, depth, width), jnp.bfloat16),
            jax.ShapeDtypeStruct((res, chans, depth), jnp.bfloat16),
            jax.ShapeDtypeStruct((res, chans, depth), jnp.bfloat16),
        ],
        scratch_shapes=[
            pltpu.VMEM((3, heads, wo.shape[0] // heads, depth), jnp.bfloat16),
            pltpu.VMEM((heads, wo.shape[0] // heads, depth), jnp.float32),
            pltpu.VMEM((heads, wo.shape[0] // heads, depth), jnp.bfloat16),
        ],
        name="column_attention",
    )(xs, mrow, mcol, gain, w_t, wo, gain2, wp_t)


def body(
    homolog_features,
    alignment_mask,
    residue_mask,
    pairwise_state,
    vertical_gain_vector,
    fourfold_projection_matrix,
    mixing_projection_matrix,
    product_gain_vector,
    product_source_matrix,
    product_target_matrix,
    outer_output_weight,
    triangle_norm_scale,
    triangle_input_weight,
    triangle_gate_weight,
    hidden_norm_scale,
    triangle_output_weight,
):
    f32, bf16 = jnp.float32, jnp.bfloat16
    groups = lax.axis_size("dap")
    me = lax.axis_index("dap")
    b = lax.axis_index("branch")
    s_loc, residues, width = homolog_features.shape
    res = residues // groups
    half = res // 2
    pair_width = pairwise_state.shape[2]

    def swap(a):
        return lax.ppermute(a, "branch", SWAP)

    def both(own, axis):
        other = swap(own)
        first = b == 0
        return jnp.concatenate([jnp.where(first, own, other), jnp.where(first, other, own)], axis=axis)

    def pick(a, axis, which):
        shape = a.shape
        a = a.reshape(shape[:axis] + (groups, 2, half) + shape[axis + 1 :])
        a = lax.dynamic_index_in_dim(a, which, axis + 1, keepdims=False)
        return a.reshape(shape[:axis] + (groups * half,) + shape[axis + 1 :])

    active = residue_mask.astype(f32)

    fourfold = both(fourfold_projection_matrix, 2)
    heads, hd = fourfold.shape[2:]
    feats = heads * hd
    w_t = fourfold.reshape(width, 4 * feats).T
    wo = both(mixing_projection_matrix.reshape(-1, width), 0)
    source = both(product_source_matrix, 1)
    chans = source.shape[1]
    wp_t = jnp.concatenate([source, product_target_matrix], axis=1).T
    outer_w = both(outer_output_weight, 0).reshape(chans * chans, pair_width)
    tri_in = both(triangle_input_weight, 2)
    hidden = tri_in.shape[2]
    tri_in = tri_in.reshape(pair_width, 4 * hidden)
    tri_gate = both(triangle_gate_weight, 1)
    hidden_gain = both(hidden_norm_scale, 0)
    tri_out = both(triangle_output_weight, 0)

    send = pick(homolog_features, 1, b).reshape(s_loc, groups, half, width).transpose(1, 2, 0, 3)
    xs = lax.all_to_all(send, "dap", split_axis=0, concat_axis=0, tiled=True)
    mask_all = lax.all_gather(alignment_mask.astype(bf16), "dap", axis=0, tiled=True)
    mask_t = (mask_all.astype(f32) * active[None, :]).T
    rows_t = lax.dynamic_slice_in_dim(mask_t, me * res, res, 0)
    own_t = lax.dynamic_slice_in_dim(mask_t, me * res + b * half, half, 0)

    mixed, left, right = column_stage(
        xs,
        own_t,
        vertical_gain_vector[None],
        w_t,
        wo,
        product_gain_vector[None],
        wp_t,
        heads,
    )
    depth = mixed.shape[1]
    left = both(left, 0).reshape(res * chans, depth)
    right = lax.all_gather(right.reshape(half * chans, depth), "dap", axis=0, tiled=True)
    homolog_mixed = both(mixed, 0).transpose(1, 0, 2)

    cols = groups * half
    outer = dot(left, right, NT).astype(bf16)
    outer = outer.reshape(res, chans, cols, chans).transpose(0, 2, 1, 3).reshape(res * cols, chans * chans)
    update = jnp.dot(outer, outer_w, preferred_element_type=f32).reshape(res, cols, pair_width)
    counts = dot(rows_t.astype(bf16), pick(mask_t, 0, b).astype(bf16), NT)
    update = update / jnp.maximum(counts, 1.0)[..., None]
    pair_mid = (pick(pairwise_state, 1, b).astype(f32) + update).astype(bf16)
    pair_field = pair_mid.astype(f32)
    pair_normed = standardize_features(pair_field, triangle_norm_scale).astype(bf16).reshape(res * cols, pair_width)
    proj = jnp.dot(pair_normed, tri_in, preferred_element_type=f32).reshape(res, cols, 4, hidden)
    row_live = lax.dynamic_slice_in_dim(active, me * res, res, 0)
    live = (row_live[:, None] * pick(active, 0, b)[None, :])[..., None]
    tri_left = (live * sigmoid(proj[:, :, 0]) * proj[:, :, 1]).astype(bf16)
    tri_right = (live * sigmoid(proj[:, :, 2]) * proj[:, :, 3]).astype(bf16)
    gate = sigmoid(jnp.dot(pair_normed, tri_gate, preferred_element_type=f32)).reshape(res, cols, pair_width)

    right_all = lax.all_gather(tri_right.transpose(0, 2, 1), "dap", axis=0, tiled=True)
    part = jnp.einsum("ick,jck->cij", tri_left.transpose(0, 2, 1), right_all, preferred_element_type=f32)
    tri_sum = pick(part, 2, b) + swap(pick(part, 2, 1 - b))
    mean_val = jnp.mean(tri_sum, axis=0, keepdims=True)
    variance = jnp.mean((tri_sum - mean_val) ** 2, axis=0, keepdims=True)
    tri_scaled = ((tri_sum - mean_val) * lax.rsqrt(variance + eps_norm) * hidden_gain[:, None, None]).astype(bf16)
    projected = dot(tri_scaled, tri_out, TN)
    out = (pair_field + gate * projected).astype(bf16)
    z_half = pair_width // 2
    own = lax.dynamic_slice_in_dim(out, b * z_half, z_half, 2)
    other = swap(lax.dynamic_slice_in_dim(out, (1 - b) * z_half, z_half, 2))
    own = own.reshape(res, groups, 1, half, z_half)
    other = other.reshape(res, groups, 1, half, z_half)
    first = b == 0
    out = jnp.concatenate([jnp.where(first, own, other), jnp.where(first, other, own)], axis=2)
    return (homolog_mixed, out.reshape(res, residues, z_half))


def solution(mesh):
    in_specs = (
        P(("crop", "dap"), None, None),
        P(("crop", "dap"), None),
        P("crop"),
        P(("crop", "dap"), None, None),
        P(),
        P(None, None, "branch", None),
        P("branch", None, None),
        P(),
        P(None, "branch"),
        P(),
        P("branch", None, None),
        P(),
        P(None, None, "branch"),
        P(None, "branch"),
        P("branch"),
        P("branch", None),
    )
    out_specs = (P("crop", "dap", None), P(("crop", "dap"), None, "branch"))
    return jax.shard_map(body, mesh=mesh, in_specs=in_specs, out_specs=out_specs, check_vma=False)
```

```python
import functools

import jax
import jax.numpy as jnp
from jax import lax
from jax.experimental import pallas as pl
from jax.experimental.pallas import tpu as pltpu
from jax.sharding import PartitionSpec as P

eps_norm = 1e-05
SWAP = ((0, 1), (1, 0))
NT = (((1,), (1,)), ((), ()))
TN = (((0,), (0,)), ((), ()))


def standardize_features(field, gain_vec):
    mean_val = jnp.mean(field, axis=-1, keepdims=True)
    variance = jnp.mean((field - mean_val) ** 2, axis=-1, keepdims=True)
    return (field - mean_val) * lax.rsqrt(variance + eps_norm) * gain_vec


def sigmoid(x):
    return 1.0 / (1.0 + jnp.exp(-x))


def dot(a, b, dims):
    return lax.dot_general(a, b, dims, preferred_element_type=jnp.float32)


def column_kernel(
    heads, x_ref, mrow_ref, mcol_ref, gain_ref, w_ref, wo_ref, gain2_ref, wp_ref, mixed_ref, left_ref, right_ref,
    qkv_ref, gate_ref, gated_ref,
):
    width = x_ref.shape[-1]
    depth = mrow_ref.shape[-1]
    feats = wo_ref.shape[0]
    hd = feats // heads
    x = x_ref[:, 0].reshape(depth, width).astype(jnp.float32)
    n = standardize_features(x, gain_ref[...]).astype(jnp.bfloat16)
    proj = dot(w_ref[...], n, NT)
    for i in range(3):
        qkv_ref[i] = proj[i * feats : (i + 1) * feats].astype(jnp.bfloat16).reshape(heads, hd, depth)
    gate_ref[...] = sigmoid(proj[3 * feats :]).reshape(heads, hd, depth)
    live = mcol_ref[0] > 0.5
    inv_root = 1.0 / hd**0.5

    def one_head(h):
        scores = dot(qkv_ref[1, h], qkv_ref[0, h], TN) * inv_root
        scores = jnp.where(live, scores, -1000000000.0)
        e = jnp.exp(scores - jnp.max(scores, axis=0, keepdims=True))
        total = jnp.sum(e, axis=0, keepdims=True)
        att = jnp.dot(qkv_ref[2, h], e.astype(jnp.bfloat16), preferred_element_type=jnp.float32)
        gated_ref[h] = (att * (1.0 / total) * gate_ref[h]).astype(jnp.bfloat16)

    unroll = 4

    @pl.loop(0, heads // unroll)
    def _(step):
        for u in range(unroll):
            one_head(step * unroll + u)

    gated = gated_ref[...].reshape(feats, depth)
    mixed = (x + dot(gated, wo_ref[...], TN)).astype(jnp.bfloat16)
    mixed_ref[0] = mixed
    n2 = standardize_features(mixed.astype(jnp.float32), gain2_ref[...]).astype(jnp.bfloat16)
    panel = (dot(wp_ref[...], n2, NT) * mrow_ref[0]).astype(jnp.bfloat16)
    chans = left_ref.shape[1]
    left_ref[0] = panel[:chans]
    right_ref[0] = panel[chans:]


def column_stage(xs, mask_rows, gain, w_t, wo, gain2, wp_t, heads):
    groups, res, s_loc, width = xs.shape
    depth = groups * s_loc
    chans = wp_t.shape[0] // 2
    whole = lambda a: pl.BlockSpec(a.shape, lambda i: (0,) * a.ndim)
    mrow = mask_rows[:, None, :]
    mcol = mask_rows[:, :, None]
    return pl.pallas_call(
        functools.partial(column_kernel, heads),
        grid=(res,),
        in_specs=[
            pl.BlockSpec((groups, 1, s_loc, width), lambda i: (0, i, 0, 0)),
            pl.BlockSpec((1, 1, depth), lambda i: (i, 0, 0)),
            pl.BlockSpec((1, depth, 1), lambda i: (i, 0, 0)),
            whole(gain),
            whole(w_t),
            whole(wo),
            whole(gain2),
            whole(wp_t),
        ],
        out_specs=[
            pl.BlockSpec((1, depth, width), lambda i: (i, 0, 0)),
            pl.BlockSpec((1, chans, depth), lambda i: (i, 0, 0)),
            pl.BlockSpec((1, chans, depth), lambda i: (i, 0, 0)),
        ],
        out_shape=[
            jax.ShapeDtypeStruct((res, depth, width), jnp.bfloat16),
            jax.ShapeDtypeStruct((res, chans, depth), jnp.bfloat16),
            jax.ShapeDtypeStruct((res, chans, depth), jnp.bfloat16),
        ],
        scratch_shapes=[
            pltpu.VMEM((3, heads, wo.shape[0] // heads, depth), jnp.bfloat16),
            pltpu.VMEM((heads, wo.shape[0] // heads, depth), jnp.float32),
            pltpu.VMEM((heads, wo.shape[0] // heads, depth), jnp.bfloat16),
        ],
        name="column_attention",
    )(xs, mrow, mcol, gain, w_t, wo, gain2, wp_t)


def remote(src, dst, send_sem, recv_sem, where):
    return pltpu.make_async_remote_copy(
        src_ref=src,
        dst_ref=dst,
        send_sem=send_sem,
        recv_sem=recv_sem,
        device_id=where,
        device_id_type=pl.DeviceIdType.MESH,
    )


def greet(places):
    barrier = pltpu.get_barrier_semaphore()
    for where in places:
        pl.semaphore_signal(barrier, inc=1, device_id=where, device_id_type=pl.DeviceIdType.MESH)
    pl.semaphore_wait(barrier, len(places))


def scatter_kernel(count, number, peer_of, slot_of, *refs):
    ins, outs = refs[:number], refs[number : 2 * number]
    send_sem, recv_sem, local_sem = refs[2 * number :]
    me = slot_of(lax.axis_index("dap"))
    greet([peer_of(lax.axis_index("dap"), d) for d in range(1, count)])
    keeps = [pltpu.make_async_copy(a.at[me], o.at[me], local_sem.at[i]) for i, (a, o) in enumerate(zip(ins, outs))]
    sends = []
    for d in range(1, count):
        place = peer_of(lax.axis_index("dap"), d)
        target = slot_of(place["dap"])
        for i, (a, o) in enumerate(zip(ins, outs)):
            copy = remote(a.at[target], o.at[me], send_sem.at[i, d], recv_sem.at[i, d], place)
            copy.start()
            sends.append(copy)
    for copy in keeps:
        copy.start()
    for d in range(1, count):
        for i, (a, o) in enumerate(zip(ins, outs)):
            source = lax.rem(me + count - d, count)
            remote(a.at[source], o.at[source], send_sem.at[i, d], recv_sem.at[i, d], peer_of(lax.axis_index("dap"), d)).wait_recv()
    for copy in sends:
        copy.wait_send()
    for copy in keeps:
        copy.wait()


def scatter(arrays, count, peer_of, slot_of, ident, name):
    number = len(arrays)
    return pl.pallas_call(
        functools.partial(scatter_kernel, count, number, peer_of, slot_of),
        in_specs=[pl.BlockSpec(memory_space=pl.ANY)] * number,
        out_specs=[pl.BlockSpec(memory_space=pl.ANY)] * number,
        out_shape=[jax.ShapeDtypeStruct(a.shape, a.dtype) for a in arrays],
        scratch_shapes=[
            pltpu.SemaphoreType.DMA((number, count)),
            pltpu.SemaphoreType.DMA((number, count)),
            pltpu.SemaphoreType.DMA((number,)),
        ],
        compiler_params=pltpu.CompilerParams(collective_id=ident, has_side_effects=True),
        name=name,
    )(*arrays)


def block_kernel(
    ny, nz, share, l_ref, r_ref, lg_ref, rg_ref, fsend, frecv, bsend, brecv, ysend, yrecv, ssend, srecv, local_sem
):
    me = lax.axis_index("dap")
    core = lax.axis_index("branch")
    y, z = me // nz, lax.rem(me, nz)
    up = {"dap": y * nz + lax.rem(z + 1, nz)}
    down = {"dap": y * nz + lax.rem(z + nz - 1, nz)}
    column = [{"dap": lax.rem(y + d, ny) * nz + z} for d in range(1, ny)]
    twin = {"branch": 1 - core}
    greet([up, down] + column + ([twin] if share else []))
    fwd, bwd = nz // 2, nz - 1 - nz // 2

    def slot(which, place):
        return lg_ref.at[which, place] if share else lg_ref.at[place]

    def at(shift):
        return lax.rem(z + nz + shift, nz)

    def ahead(t):
        return remote(l_ref if t == 0 else slot(core, at(-t)), slot(core, at(-t)), fsend.at[t], frecv.at[t], up)

    def back(t):
        return remote(l_ref if t == 0 else slot(core, at(t)), slot(core, at(t)), bsend.at[t], brecv.at[t], down)

    def ahead_in(t):
        return remote(l_ref, slot(core, at(-1 - t)), fsend.at[t], frecv.at[t], up)

    def back_in(t):
        return remote(l_ref, slot(core, at(1 + t)), bsend.at[t], brecv.at[t], down)

    def pass_on(i, shift):
        return remote(l_ref if shift == 0 else slot(core, at(shift)), slot(core, at(shift)), ssend.at[i], srecv.at[i], twin)

    shifts = [0]
    sends = [ahead(0)] + ([back(0)] if bwd else [])
    sends += [remote(r_ref, rg_ref.at[y], ysend.at[d], yrecv.at[d], column[d]) for d in range(ny - 1)]
    if share:
        sends.append(pass_on(0, 0))
    for copy in sends:
        copy.start()
    keeps = [
        pltpu.make_async_copy(l_ref, slot(core, z), local_sem.at[0]),
        pltpu.make_async_copy(r_ref, rg_ref.at[y], local_sem.at[1]),
    ]
    for copy in keeps:
        copy.start()

    def follow(copy):
        copy.start()
        sends.append(copy)

    for t in range(fwd):
        ahead_in(t).wait_recv()
        if t + 1 < fwd:
            follow(ahead(t + 1))
        if share:
            shifts.append(-1 - t)
            follow(pass_on(len(shifts) - 1, -1 - t))
        if t < bwd:
            back_in(t).wait_recv()
            if t + 1 < bwd:
                follow(back(t + 1))
            if share:
                shifts.append(1 + t)
                follow(pass_on(len(shifts) - 1, 1 + t))
    for d in range(ny - 1):
        remote(r_ref, rg_ref.at[lax.rem(y + ny - 1 - d, ny)], ysend.at[d], yrecv.at[d], column[d]).wait_recv()
    if share:
        for i, shift in enumerate(shifts):
            remote(l_ref, slot(1 - core, at(shift)), ssend.at[i], srecv.at[i], twin).wait_recv()
    for copy in sends:
        copy.wait_send()
    for copy in keeps:
        copy.wait()


def gather_blocks(left, right, ny, nz, share, ident, name):
    sems = lambda n: pltpu.SemaphoreType.DMA((n,))
    lead = (2, nz) if share else (nz,)
    return pl.pallas_call(
        functools.partial(block_kernel, ny, nz, share),
        in_specs=[pl.BlockSpec(memory_space=pl.ANY)] * 2,
        out_specs=[pl.BlockSpec(memory_space=pl.ANY)] * 2,
        out_shape=[
            jax.ShapeDtypeStruct(lead + left.shape, left.dtype),
            jax.ShapeDtypeStruct((ny,) + right.shape, right.dtype),
        ],
        scratch_shapes=[sems(nz), sems(nz), sems(nz), sems(nz), sems(ny), sems(ny), sems(nz), sems(nz), sems(2)],
        compiler_params=pltpu.CompilerParams(collective_id=ident, has_side_effects=True),
        name=name,
    )(left, right)


def body(
    homolog_features,
    alignment_mask,
    residue_mask,
    pairwise_state,
    vertical_gain_vector,
    fourfold_projection_matrix,
    mixing_projection_matrix,
    product_gain_vector,
    product_source_matrix,
    product_target_matrix,
    outer_output_weight,
    triangle_norm_scale,
    triangle_input_weight,
    triangle_gate_weight,
    hidden_norm_scale,
    triangle_output_weight,
):
    f32, bf16 = jnp.float32, jnp.bfloat16
    groups = lax.axis_size("dap")
    me = lax.axis_index("dap")
    b = lax.axis_index("branch")
    s_loc, residues, width = homolog_features.shape
    res = residues // groups
    half = res // 2
    pair_width = pairwise_state.shape[2]

    def swap(a):
        return lax.ppermute(a, "branch", SWAP)

    def both(own, axis):
        other = swap(own)
        first = b == 0
        return jnp.concatenate([jnp.where(first, own, other), jnp.where(first, other, own)], axis=axis)

    def pick(a, axis, which):
        shape = a.shape
        a = a.reshape(shape[:axis] + (groups, 2, half) + shape[axis + 1 :])
        a = lax.dynamic_index_in_dim(a, which, axis + 1, keepdims=False)
        return a.reshape(shape[:axis] + (groups * half,) + shape[axis + 1 :])

    active = residue_mask.astype(f32)

    fourfold = both(fourfold_projection_matrix, 2)
    heads, hd = fourfold.shape[2:]
    feats = heads * hd
    w_t = fourfold.reshape(width, 4 * feats).T
    wo = both(mixing_projection_matrix.reshape(-1, width), 0)
    source = both(product_source_matrix, 1)
    chans = source.shape[1]
    wp_t = jnp.concatenate([source, product_target_matrix], axis=1).T
    outer_w = both(outer_output_weight, 0).reshape(chans * chans, pair_width)
    tri_in = both(triangle_input_weight, 2)
    hidden = tri_in.shape[2]
    tri_in = tri_in.reshape(pair_width, 4 * hidden)
    tri_gate = both(triangle_gate_weight, 1)
    hidden_gain = both(hidden_norm_scale, 0)
    tri_out = both(triangle_output_weight, 0)

    ny = 4 if groups % 16 == 0 else 2
    nz = groups // ny
    row = lambda i: i - lax.rem(i, nz)
    row_peer = lambda i, d: {"dap": row(i) + lax.rem(lax.rem(i, nz) + d, nz)}
    row_slot = lambda i: lax.rem(i, nz)
    all_peer = lambda i, d: {"dap": lax.rem(i + d, groups)}

    send = pick(homolog_features, 1, b).reshape(s_loc, groups, half, width).transpose(1, 2, 0, 3)
    own_mask = pick(alignment_mask.astype(bf16), 1, b).reshape(s_loc, groups, half).transpose(1, 2, 0)
    own_mask = jnp.pad(own_mask, ((0, 0), (0, 8 - half), (0, 128 - s_loc)))
    xs, mask_in = scatter([send, own_mask], groups, all_peer, lambda i: i, 1, "feature_exchange")
    depth = groups * s_loc
    mask_in = mask_in[:, :half, :s_loc].transpose(1, 0, 2).reshape(half, depth).astype(f32)
    own_active = lax.dynamic_slice_in_dim(active, me * res + b * half, half, 0)
    own_t = mask_in * own_active[:, None]

    mixed, left, right = column_stage(
        xs,
        own_t,
        vertical_gain_vector[None],
        w_t,
        wo,
        product_gain_vector[None],
        wp_t,
        heads,
    )
    tail = jnp.pad(own_t.astype(bf16), ((0, 8 - half), (0, 0)))
    left = jnp.concatenate([left.reshape(half * chans, depth), tail], axis=0)
    right = jnp.concatenate([right.reshape(half * chans, depth), tail], axis=0)
    left, right = gather_blocks(left, right, ny, nz, True, 2, "panel_gather")
    homolog_mixed = both(mixed, 0).transpose(1, 0, 2)

    panel_rows = half * chans
    rows_i, cols_j = 2 * nz * half, ny * half
    outer = dot(
        left[:, :, :panel_rows].reshape(rows_i * chans, depth), right[:, :panel_rows].reshape(cols_j * chans, depth), NT
    ).astype(bf16)
    outer = outer.reshape(rows_i, chans, cols_j, chans).transpose(0, 2, 1, 3).reshape(rows_i * cols_j, chans * chans)
    update = jnp.dot(outer, outer_w, preferred_element_type=f32).reshape(rows_i, cols_j, pair_width)
    counts = dot(
        left[:, :, panel_rows : panel_rows + half].reshape(rows_i, depth),
        right[:, panel_rows : panel_rows + half].reshape(cols_j, depth),
        NT,
    )
    update = (update / jnp.maximum(counts, 1.0)[..., None]).astype(bf16)
    update = update.reshape(2, nz, half, cols_j, pair_width).transpose(1, 0, 2, 3, 4)
    (update,) = scatter([update.reshape(nz, res, cols_j, pair_width)], nz, row_peer, row_slot, 3, "update_exchange")

    def arrange(a):
        a = a.reshape(a.shape[:1] + (ny, nz, 2, half) + a.shape[2:])
        a = lax.dynamic_index_in_dim(a, b, 3, keepdims=False)
        return jnp.swapaxes(a, 1, 2).reshape((a.shape[0], groups * half) + a.shape[4:])

    cols = groups * half
    update = update.transpose(1, 0, 2, 3).reshape(res, cols, pair_width).astype(f32)
    pair_mid = (arrange(pairwise_state).astype(f32) + update).astype(bf16)
    pair_field = pair_mid.astype(f32)
    pair_normed = standardize_features(pair_field, triangle_norm_scale).astype(bf16).reshape(res * cols, pair_width)
    proj = jnp.dot(pair_normed, tri_in, preferred_element_type=f32).reshape(res, cols, 4, hidden)
    row_live = lax.dynamic_slice_in_dim(active, me * res, res, 0)
    live = (row_live[:, None] * arrange(active[None])[0][None, :])[..., None]
    tri_left = (live * sigmoid(proj[:, :, 0]) * proj[:, :, 1]).astype(bf16)
    tri_right = (live * sigmoid(proj[:, :, 2]) * proj[:, :, 3]).astype(bf16)
    gate = sigmoid(jnp.dot(pair_normed, tri_gate, preferred_element_type=f32)).reshape(res, cols, pair_width)

    tri_left, tri_right = gather_blocks(
        tri_left.transpose(2, 0, 1), tri_right.transpose(2, 0, 1), ny, nz, False, 4, "triangle_gather"
    )
    tri_left = tri_left.transpose(1, 0, 2, 3).reshape(hidden, nz * res, cols)
    tri_right = tri_right.reshape(ny, hidden, 2, half, cols).transpose(2, 1, 0, 3, 4).reshape(2, hidden, cols_j, cols)

    def share_of(which):
        chosen = lax.dynamic_index_in_dim(tri_right, which, 0, keepdims=False)
        return jnp.einsum("cik,cjk->cij", tri_left, chosen, preferred_element_type=f32)

    given = swap(share_of(1 - b))
    tri_sum = share_of(b) + given
    mean_val = jnp.mean(tri_sum, axis=0, keepdims=True)
    variance = jnp.mean((tri_sum - mean_val) ** 2, axis=0, keepdims=True)
    tri_scaled = ((tri_sum - mean_val) * lax.rsqrt(variance + eps_norm) * hidden_gain[:, None, None]).astype(bf16)
    projected = dot(tri_scaled, tri_out, TN).astype(bf16)
    (projected,) = scatter(
        [projected.reshape(nz, res, cols_j, pair_width)], nz, row_peer, row_slot, 5, "triangle_exchange"
    )
    projected = projected.transpose(1, 0, 2, 3).reshape(res, cols, pair_width).astype(f32)
    out = (pair_field + gate * projected).astype(bf16)
    z_half = pair_width // 2
    own = lax.dynamic_slice_in_dim(out, b * z_half, z_half, 2)
    other = swap(lax.dynamic_slice_in_dim(out, (1 - b) * z_half, z_half, 2))
    own = own.reshape(res, nz, ny, 1, half, z_half)
    other = other.reshape(res, nz, ny, 1, half, z_half)
    first = b == 0
    out = jnp.concatenate([jnp.where(first, own, other), jnp.where(first, other, own)], axis=3)
    return (homolog_mixed, jnp.swapaxes(out, 1, 2).reshape(res, residues, z_half))


def solution(mesh):
    in_specs = (
        P(("crop", "dap"), None, None),
        P(("crop", "dap"), None),
        P("crop"),
        P(("crop", "dap"), None, None),
        P(),
        P(None, None, "branch", None),
        P("branch", None, None),
        P(),
        P(None, "branch"),
        P(),
        P("branch", None, None),
        P(),
        P(None, None, "branch"),
        P(None, "branch"),
        P("branch"),
        P("branch", None),
    )
    out_specs = (P("crop", "dap", None), P(("crop", "dap"), None, "branch"))
    return jax.shard_map(body, mesh=mesh, in_specs=in_specs, out_specs=out_specs, check_vma=False)
```

```python
import functools

import jax
import jax.numpy as jnp
from jax import lax
from jax.experimental import pallas as pl
from jax.experimental.pallas import tpu as pltpu
from jax.sharding import PartitionSpec as P

eps_norm = 1e-05
SWAP = ((0, 1), (1, 0))
NT = (((1,), (1,)), ((), ()))
TN = (((0,), (0,)), ((), ()))


def standardize_features(field, gain_vec):
    mean_val = jnp.mean(field, axis=-1, keepdims=True)
    variance = jnp.mean((field - mean_val) ** 2, axis=-1, keepdims=True)
    return (field - mean_val) * lax.rsqrt(variance + eps_norm) * gain_vec


def sigmoid(x):
    return 1.0 / (1.0 + jnp.exp(-x))


def dot(a, b, dims):
    return lax.dot_general(a, b, dims, preferred_element_type=jnp.float32)


def remote(src, dst, send_sem, recv_sem, where):
    return pltpu.make_async_remote_copy(
        src_ref=src,
        dst_ref=dst,
        send_sem=send_sem,
        recv_sem=recv_sem,
        device_id=where,
        device_id_type=pl.DeviceIdType.MESH,
    )


def greet(places):
    barrier = pltpu.get_barrier_semaphore()
    for where in places:
        pl.semaphore_signal(barrier, inc=1, device_id=where, device_id_type=pl.DeviceIdType.MESH)
    pl.semaphore_wait(barrier, len(places))


def scatter_kernel(count, number, peer_of, slot_of, *refs):
    ins, outs = refs[:number], refs[number : 2 * number]
    send_sem, recv_sem, local_sem = refs[2 * number :]
    me = slot_of(lax.axis_index("dap"))
    greet([peer_of(lax.axis_index("dap"), d) for d in range(1, count)])
    keeps = [pltpu.make_async_copy(a.at[me], o.at[me], local_sem.at[i]) for i, (a, o) in enumerate(zip(ins, outs))]
    sends = []
    for d in range(1, count):
        place = peer_of(lax.axis_index("dap"), d)
        target = slot_of(place["dap"])
        for i, (a, o) in enumerate(zip(ins, outs)):
            copy = remote(a.at[target], o.at[me], send_sem.at[i, d], recv_sem.at[i, d], place)
            copy.start()
            sends.append(copy)
    for copy in keeps:
        copy.start()
    for d in range(1, count):
        for i, (a, o) in enumerate(zip(ins, outs)):
            source = lax.rem(me + count - d, count)
            remote(a.at[source], o.at[source], send_sem.at[i, d], recv_sem.at[i, d], peer_of(lax.axis_index("dap"), d)).wait_recv()
    for copy in sends:
        copy.wait_send()
    for copy in keeps:
        copy.wait()


def scatter(arrays, count, peer_of, slot_of, ident, name):
    number = len(arrays)
    return pl.pallas_call(
        functools.partial(scatter_kernel, count, number, peer_of, slot_of),
        in_specs=[pl.BlockSpec(memory_space=pl.ANY)] * number,
        out_specs=[pl.BlockSpec(memory_space=pl.ANY)] * number,
        out_shape=[jax.ShapeDtypeStruct(a.shape, a.dtype) for a in arrays],
        scratch_shapes=[
            pltpu.SemaphoreType.DMA((number, count)),
            pltpu.SemaphoreType.DMA((number, count)),
            pltpu.SemaphoreType.DMA((number,)),
        ],
        compiler_params=pltpu.CompilerParams(collective_id=ident, has_side_effects=True),
        name=name,
    )(*arrays)


def block_kernel(
    ny, nz, share, l_ref, r_ref, lg_ref, rg_ref, fsend, frecv, bsend, brecv, ysend, yrecv, ssend, srecv, local_sem
):
    me = lax.axis_index("dap")
    core = lax.axis_index("branch")
    y, z = me // nz, lax.rem(me, nz)
    up = {"dap": y * nz + lax.rem(z + 1, nz)}
    down = {"dap": y * nz + lax.rem(z + nz - 1, nz)}
    column = [{"dap": lax.rem(y + d, ny) * nz + z} for d in range(1, ny)]
    twin = {"branch": 1 - core}
    greet([up, down] + column + ([twin] if share else []))
    fwd, bwd = nz // 2, nz - 1 - nz // 2

    def slot(which, place):
        return lg_ref.at[which, place] if share else lg_ref.at[place]

    def at(shift):
        return lax.rem(z + nz + shift, nz)

    def ahead(t):
        return remote(l_ref if t == 0 else slot(core, at(-t)), slot(core, at(-t)), fsend.at[t], frecv.at[t], up)

    def back(t):
        return remote(l_ref if t == 0 else slot(core, at(t)), slot(core, at(t)), bsend.at[t], brecv.at[t], down)

    def ahead_in(t):
        return remote(l_ref, slot(core, at(-1 - t)), fsend.at[t], frecv.at[t], up)

    def back_in(t):
        return remote(l_ref, slot(core, at(1 + t)), bsend.at[t], brecv.at[t], down)

    def pass_on(i, shift):
        return remote(l_ref if shift == 0 else slot(core, at(shift)), slot(core, at(shift)), ssend.at[i], srecv.at[i], twin)

    shifts = [0]
    sends = [ahead(0)] + ([back(0)] if bwd else [])
    sends += [remote(r_ref, rg_ref.at[y], ysend.at[d], yrecv.at[d], column[d]) for d in range(ny - 1)]
    if share:
        sends.append(pass_on(0, 0))
    for copy in sends:
        copy.start()
    keeps = [
        pltpu.make_async_copy(l_ref, slot(core, z), local_sem.at[0]),
        pltpu.make_async_copy(r_ref, rg_ref.at[y], local_sem.at[1]),
    ]
    for copy in keeps:
        copy.start()

    def follow(copy):
        copy.start()
        sends.append(copy)

    for t in range(fwd):
        ahead_in(t).wait_recv()
        if t + 1 < fwd:
            follow(ahead(t + 1))
        if share:
            shifts.append(-1 - t)
            follow(pass_on(len(shifts) - 1, -1 - t))
        if t < bwd:
            back_in(t).wait_recv()
            if t + 1 < bwd:
                follow(back(t + 1))
            if share:
                shifts.append(1 + t)
                follow(pass_on(len(shifts) - 1, 1 + t))
    for d in range(ny - 1):
        remote(r_ref, rg_ref.at[lax.rem(y + ny - 1 - d, ny)], ysend.at[d], yrecv.at[d], column[d]).wait_recv()
    if share:
        for i, shift in enumerate(shifts):
            remote(l_ref, slot(1 - core, at(shift)), ssend.at[i], srecv.at[i], twin).wait_recv()
    for copy in sends:
        copy.wait_send()
    for copy in keeps:
        copy.wait()


def gather_blocks(left, right, ny, nz, share, ident, name):
    sems = lambda n: pltpu.SemaphoreType.DMA((n,))
    lead = (2, nz) if share else (nz,)
    return pl.pallas_call(
        functools.partial(block_kernel, ny, nz, share),
        in_specs=[pl.BlockSpec(memory_space=pl.ANY)] * 2,
        out_specs=[pl.BlockSpec(memory_space=pl.ANY)] * 2,
        out_shape=[
            jax.ShapeDtypeStruct(lead + left.shape, left.dtype),
            jax.ShapeDtypeStruct((ny,) + right.shape, right.dtype),
        ],
        scratch_shapes=[sems(nz), sems(nz), sems(nz), sems(nz), sems(ny), sems(ny), sems(nz), sems(nz), sems(2)],
        compiler_params=pltpu.CompilerParams(collective_id=ident, has_side_effects=True),
        name=name,
    )(left, right)


def column_kernel(
    heads, number, send_ref, msend_ref, gain_ref, gain2_ref, w_ref, wo_ref, ws_ref, wt_ref, *refs
):
    extras, (mixed_ref, left_ref, right_ref), both_refs = refs[:number], refs[number : number + 3], refs[number + 3 : 2 * number + 3]
    (
        x_ref, m_ref, w2_ref, wo2_ref, ws2_ref, qkv_ref, gate_ref, gated_ref,
        send_sem, recv_sem, msend_sem, mrecv_sem, keep_sem, tsend_sem, trecv_sem, tkeep_sem,
    ) = refs[2 * number + 3 :]
    res, count, s_loc, width = send_ref.shape
    depth = count * s_loc
    feats = wo2_ref.shape[0] * wo2_ref.shape[1]
    hd = feats // heads
    part = feats // 2
    me = lax.axis_index("dap")
    core = lax.axis_index("branch")
    twin = {"branch": 1 - core}
    barrier = pltpu.get_barrier_semaphore()

    def hello(d, carry):
        pl.semaphore_signal(
            barrier, inc=1, device_id={"dap": lax.rem(me + d, count)}, device_id_type=pl.DeviceIdType.MESH
        )
        return carry

    lax.fori_loop(1, count, hello, 0)
    pl.semaphore_signal(barrier, inc=1, device_id=twin, device_id_type=pl.DeviceIdType.MESH)
    pl.semaphore_wait(barrier, count)

    def give_mask(d, carry):
        peer = lax.rem(me + d, count)
        remote(msend_ref.at[peer], m_ref.at[me], msend_sem.at[0], mrecv_sem.at[0], {"dap": peer}).start()
        return carry

    lax.fori_loop(1, count, give_mask, 0)
    pairs = [(w_ref, w2_ref), (wo_ref, wo2_ref), (ws_ref, ws2_ref)] + list(zip(extras, both_refs))
    swaps = [remote(a, o.at[core], tsend_sem.at[i], trecv_sem.at[i], twin) for i, (a, o) in enumerate(pairs)]
    for copy in swaps:
        copy.start()
    for r in range(res):

        def give(d, carry):
            peer = lax.rem(me + d, count)
            remote(send_ref.at[r, peer], x_ref.at[r, me], send_sem.at[r], recv_sem.at[r], {"dap": peer}).start()
            return carry

        lax.fori_loop(1, count, give, 0)
    keeps = [pltpu.make_async_copy(a, o.at[core], tkeep_sem.at[i]) for i, (a, o) in enumerate(pairs)]
    keeps += [pltpu.make_async_copy(send_ref.at[r, me], x_ref.at[r, me], keep_sem.at[r]) for r in range(res)]
    keeps.append(pltpu.make_async_copy(msend_ref.at[me], m_ref.at[me], keep_sem.at[res]))
    for copy in keeps:
        copy.start()
    for copy in keeps:
        copy.wait()
    for i, (a, o) in enumerate(pairs):
        remote(a, o.at[1 - core], tsend_sem.at[i], trecv_sem.at[i], twin).wait_recv()
    rest = pl.ds(0, count - 1)
    masks = remote(msend_ref.at[rest], m_ref.at[rest], msend_sem.at[0], mrecv_sem.at[0], twin)
    masks.wait_recv()

    m = m_ref[...].reshape(depth, 128)
    rows = lax.broadcasted_iota(jnp.int32, (8, 128), 0)
    lanes = lax.broadcasted_iota(jnp.int32, (8, 128), 1)
    tail = dot((rows == lanes).astype(jnp.bfloat16), m, NT).astype(jnp.bfloat16)
    chans = wt_ref.shape[0]
    left_ref[res * chans :] = tail
    right_ref[res * chans :] = tail
    inv_root = 1.0 / hd**0.5

    @pl.loop(0, res)
    def _(r):
        remote(send_ref.at[r, rest], x_ref.at[r, rest], send_sem.at[r], recv_sem.at[r], twin).wait_recv()
        x = x_ref[r].reshape(depth, width).astype(jnp.float32)
        n = standardize_features(x, gain_ref[...]).astype(jnp.bfloat16)
        for c in range(2):
            proj = dot(w2_ref[c], n, NT)
            for i in range(3):
                qkv_ref[i, c * (heads // 2) : (c + 1) * (heads // 2)] = (
                    proj[i * part : (i + 1) * part].astype(jnp.bfloat16).reshape(heads // 2, hd, depth)
                )
            gate_ref[c * (heads // 2) : (c + 1) * (heads // 2)] = sigmoid(proj[3 * part :]).reshape(heads // 2, hd, depth)
        lane = lax.broadcasted_iota(jnp.int32, (depth, 128), 1)
        mcol = jnp.sum(jnp.where(lane == r, m_ref[...].reshape(depth, 128).astype(jnp.float32), 0.0), axis=1, keepdims=True)
        live = mcol > 0.5

        def one_head(h):
            scores = dot(qkv_ref[1, h], qkv_ref[0, h], TN) * inv_root
            scores = jnp.where(live, scores, -1000000000.0)
            e = jnp.exp(scores - jnp.max(scores, axis=0, keepdims=True))
            total = jnp.sum(e, axis=0, keepdims=True)
            att = jnp.dot(qkv_ref[2, h], e.astype(jnp.bfloat16), preferred_element_type=jnp.float32)
            gated_ref[h] = (att * (1.0 / total) * gate_ref[h]).astype(jnp.bfloat16)

        unroll = 4

        @pl.loop(0, heads // unroll)
        def _(step):
            for u in range(unroll):
                one_head(step * unroll + u)

        gated = gated_ref[...].reshape(feats, depth)
        mixed = (x + dot(gated, wo2_ref[...].reshape(feats, width), TN)).astype(jnp.bfloat16)
        mixed_ref[r] = mixed
        n2 = standardize_features(mixed.astype(jnp.float32), gain2_ref[...]).astype(jnp.bfloat16)
        mrow = dot((lanes == r).astype(jnp.bfloat16), m_ref[...].reshape(depth, 128), NT)[:1]
        where = pl.ds(pl.multiple_of(r * chans, chans), chans)
        left_ref[where] = (dot(ws2_ref[...].reshape(chans, width), n2, NT) * mrow).astype(jnp.bfloat16)
        right_ref[where] = (dot(wt_ref[...], n2, NT) * mrow).astype(jnp.bfloat16)

    for copy in swaps:
        copy.wait_send()
    masks.wait_send()
    for r in range(res):
        remote(send_ref.at[r, rest], x_ref.at[r, rest], send_sem.at[r], recv_sem.at[r], twin).wait_send()


def column_stage(send, msend, gain, gain2, w_t, wo, ws_t, wt_t, extras, heads):
    res, groups, s_loc, width = send.shape
    depth = groups * s_loc
    chans = wt_t.shape[0]
    number = len(extras)
    feats = 2 * wo.shape[0]
    hd = feats // heads
    vmem = pl.BlockSpec(memory_space=pltpu.VMEM)
    hbm = pl.BlockSpec(memory_space=pl.ANY)
    bf16 = jnp.bfloat16
    panel = jax.ShapeDtypeStruct((res * chans + 8, depth), bf16)
    return pl.pallas_call(
        functools.partial(column_kernel, heads, number),
        in_specs=[hbm, hbm] + [vmem] * 6 + [hbm] * number,
        out_specs=[vmem] * 3 + [hbm] * number,
        out_shape=[jax.ShapeDtypeStruct((res, depth, width), bf16), panel, panel]
        + [jax.ShapeDtypeStruct((2,) + a.shape, a.dtype) for a in extras],
        scratch_shapes=[
            pltpu.VMEM(send.shape, bf16),
            pltpu.VMEM(msend.shape, bf16),
            pltpu.VMEM((2,) + w_t.shape, bf16),
            pltpu.VMEM((2,) + wo.shape, bf16),
            pltpu.VMEM((2,) + ws_t.shape, bf16),
            pltpu.VMEM((3, heads, hd, depth), bf16),
            pltpu.VMEM((heads, hd, depth), jnp.float32),
            pltpu.VMEM((heads, hd, depth), bf16),
            pltpu.SemaphoreType.DMA((res,)),
            pltpu.SemaphoreType.DMA((res,)),
            pltpu.SemaphoreType.DMA((1,)),
            pltpu.SemaphoreType.DMA((1,)),
            pltpu.SemaphoreType.DMA((res + 1,)),
            pltpu.SemaphoreType.DMA((3 + number,)),
            pltpu.SemaphoreType.DMA((3 + number,)),
            pltpu.SemaphoreType.DMA((3 + number,)),
        ],
        compiler_params=pltpu.CompilerParams(collective_id=1, has_side_effects=True),
        name="column_attention",
    )(send, msend, gain, gain2, w_t, wo, ws_t, wt_t, *extras)


def body(
    homolog_features,
    alignment_mask,
    residue_mask,
    pairwise_state,
    vertical_gain_vector,
    fourfold_projection_matrix,
    mixing_projection_matrix,
    product_gain_vector,
    product_source_matrix,
    product_target_matrix,
    outer_output_weight,
    triangle_norm_scale,
    triangle_input_weight,
    triangle_gate_weight,
    hidden_norm_scale,
    triangle_output_weight,
):
    f32, bf16 = jnp.float32, jnp.bfloat16
    groups = lax.axis_size("dap")
    me = lax.axis_index("dap")
    b = lax.axis_index("branch")
    s_loc, residues, width = homolog_features.shape
    res = residues // groups
    half = res // 2
    pair_width = pairwise_state.shape[2]

    def swap(a):
        return lax.ppermute(a, "branch", SWAP)

    def both(own, axis):
        other = swap(own)
        first = b == 0
        return jnp.concatenate([jnp.where(first, own, other), jnp.where(first, other, own)], axis=axis)

    def pick(a, axis, which):
        shape = a.shape
        a = a.reshape(shape[:axis] + (groups, 2, half) + shape[axis + 1 :])
        a = lax.dynamic_index_in_dim(a, which, axis + 1, keepdims=False)
        return a.reshape(shape[:axis] + (groups * half,) + shape[axis + 1 :])

    active = residue_mask.astype(f32)

    heads, hd = 2 * fourfold_projection_matrix.shape[2], fourfold_projection_matrix.shape[3]
    w_t = fourfold_projection_matrix.reshape(width, -1).T
    wo = mixing_projection_matrix.reshape(-1, width)
    chans = product_target_matrix.shape[1]
    hidden = 2 * triangle_input_weight.shape[2]
    extras = [
        outer_output_weight.reshape(-1, pair_width),
        triangle_input_weight.transpose(1, 2, 0),
        triangle_gate_weight.T,
        triangle_output_weight,
        jnp.broadcast_to(hidden_norm_scale[None], (8, hidden // 2)),
    ]

    ny = 4 if groups % 16 == 0 else 2
    nz = groups // ny
    row = lambda i: i - lax.rem(i, nz)
    row_peer = lambda i, d: {"dap": row(i) + lax.rem(lax.rem(i, nz) + d, nz)}
    row_slot = lambda i: lax.rem(i, nz)

    send = pick(homolog_features, 1, b).reshape(s_loc, groups, half, width).transpose(2, 1, 0, 3)
    own_mask = pick((alignment_mask * residue_mask[None, :]).astype(bf16), 1, b)
    own_mask = own_mask.reshape(s_loc, groups, half).transpose(1, 0, 2)
    own_mask = jnp.pad(own_mask, ((0, 0), (0, 0), (0, 128 - half)))
    depth = groups * s_loc
    mixed, left, right, outer_w, tri_in, tri_gate, tri_out, hidden_gain = column_stage(
        send,
        own_mask,
        vertical_gain_vector[None],
        product_gain_vector[None],
        w_t,
        wo,
        product_source_matrix.T,
        product_target_matrix.T,
        extras,
        heads,
    )
    outer_w = outer_w.reshape(chans * chans, pair_width)
    tri_in = tri_in.transpose(1, 0, 2, 3).reshape(4 * hidden, pair_width).T
    tri_gate = tri_gate.reshape(pair_width, pair_width).T
    tri_out = tri_out.reshape(hidden, pair_width)
    hidden_gain = hidden_gain[:, 0].reshape(hidden)
    left, right = gather_blocks(left, right, ny, nz, True, 2, "panel_gather")
    homolog_mixed = both(mixed, 0).transpose(1, 0, 2)

    panel_rows = half * chans
    rows_i, cols_j = 2 * nz * half, ny * half
    outer = dot(
        left[:, :, :panel_rows].reshape(rows_i * chans, depth), right[:, :panel_rows].reshape(cols_j * chans, depth), NT
    ).astype(bf16)
    outer = outer.reshape(rows_i, chans, cols_j, chans).transpose(0, 2, 1, 3).reshape(rows_i * cols_j, chans * chans)
    update = jnp.dot(outer, outer_w, preferred_element_type=f32).reshape(rows_i, cols_j, pair_width)
    counts = dot(
        left[:, :, panel_rows : panel_rows + half].reshape(rows_i, depth),
        right[:, panel_rows : panel_rows + half].reshape(cols_j, depth),
        NT,
    )
    update = (update / jnp.maximum(counts, 1.0)[..., None]).astype(bf16)
    update = update.reshape(2, nz, half, cols_j, pair_width).transpose(1, 0, 2, 3, 4)
    (update,) = scatter([update.reshape(nz, res, cols_j, pair_width)], nz, row_peer, row_slot, 3, "update_exchange")

    def arrange(a):
        a = a.reshape(a.shape[:1] + (ny, nz, 2, half) + a.shape[2:])
        a = lax.dynamic_index_in_dim(a, b, 3, keepdims=False)
        return jnp.swapaxes(a, 1, 2).reshape((a.shape[0], groups * half) + a.shape[4:])

    cols = groups * half
    update = update.transpose(1, 0, 2, 3).reshape(res, cols, pair_width).astype(f32)
    pair_mid = (arrange(pairwise_state).astype(f32) + update).astype(bf16)
    pair_field = pair_mid.astype(f32)
    pair_normed = standardize_features(pair_field, triangle_norm_scale).astype(bf16).reshape(res * cols, pair_width)
    proj = jnp.dot(pair_normed, tri_in, preferred_element_type=f32).reshape(res, cols, 4, hidden)
    row_live = lax.dynamic_slice_in_dim(active, me * res, res, 0)
    live = (row_live[:, None] * arrange(active[None])[0][None, :])[..., None]
    tri_left = (live * sigmoid(proj[:, :, 0]) * proj[:, :, 1]).astype(bf16)
    tri_right = (live * sigmoid(proj[:, :, 2]) * proj[:, :, 3]).astype(bf16)
    gate = sigmoid(jnp.dot(pair_normed, tri_gate, preferred_element_type=f32)).reshape(res, cols, pair_width)

    tri_left, tri_right = gather_blocks(
        tri_left.transpose(2, 0, 1), tri_right.transpose(2, 0, 1), ny, nz, False, 4, "triangle_gather"
    )
    tri_left = tri_left.transpose(1, 0, 2, 3).reshape(hidden, nz * res, cols)
    tri_right = tri_right.reshape(ny, hidden, 2, half, cols).transpose(2, 1, 0, 3, 4).reshape(2, hidden, cols_j, cols)

    def share_of(which):
        chosen = lax.dynamic_index_in_dim(tri_right, which, 0, keepdims=False)
        return jnp.einsum("cik,cjk->cij", tri_left, chosen, preferred_element_type=f32)

    given = swap(share_of(1 - b))
    tri_sum = share_of(b) + given
    mean_val = jnp.mean(tri_sum, axis=0, keepdims=True)
    variance = jnp.mean((tri_sum - mean_val) ** 2, axis=0, keepdims=True)
    tri_scaled = ((tri_sum - mean_val) * lax.rsqrt(variance + eps_norm) * hidden_gain[:, None, None]).astype(bf16)
    projected = dot(tri_scaled, tri_out, TN).astype(bf16)
    (projected,) = scatter(
        [projected.reshape(nz, res, cols_j, pair_width)], nz, row_peer, row_slot, 5, "triangle_exchange"
    )
    projected = projected.transpose(1, 0, 2, 3).reshape(res, cols, pair_width).astype(f32)
    out = (pair_field + gate * projected).astype(bf16)
    z_half = pair_width // 2
    own = lax.dynamic_slice_in_dim(out, b * z_half, z_half, 2)
    other = swap(lax.dynamic_slice_in_dim(out, (1 - b) * z_half, z_half, 2))
    own = own.reshape(res, nz, ny, 1, half, z_half)
    other = other.reshape(res, nz, ny, 1, half, z_half)
    first = b == 0
    out = jnp.concatenate([jnp.where(first, own, other), jnp.where(first, other, own)], axis=3)
    return (homolog_mixed, jnp.swapaxes(out, 1, 2).reshape(res, residues, z_half))


def solution(mesh):
    in_specs = (
        P(("crop", "dap"), None, None),
        P(("crop", "dap"), None),
        P("crop"),
        P(("crop", "dap"), None, None),
        P(),
        P(None, None, "branch", None),
        P("branch", None, None),
        P(),
        P(None, "branch"),
        P(),
        P("branch", None, None),
        P(),
        P(None, None, "branch"),
        P(None, "branch"),
        P("branch"),
        P("branch", None),
    )
    out_specs = (P("crop", "dap", None), P(("crop", "dap"), None, "branch"))
    return jax.shard_map(body, mesh=mesh, in_specs=in_specs, out_specs=out_specs, check_vma=False)
```

```python
import functools

import jax
import jax.numpy as jnp
from jax import lax
from jax.experimental import pallas as pl
from jax.experimental.pallas import tpu as pltpu
from jax.sharding import PartitionSpec as P

eps_norm = 1e-05
SWAP = ((0, 1), (1, 0))
NT = (((1,), (1,)), ((), ()))
TN = (((0,), (0,)), ((), ()))


def standardize_features(field, gain_vec):
    mean_val = jnp.mean(field, axis=-1, keepdims=True)
    variance = jnp.mean((field - mean_val) ** 2, axis=-1, keepdims=True)
    return (field - mean_val) * lax.rsqrt(variance + eps_norm) * gain_vec


def sigmoid(x):
    return 1.0 / (1.0 + jnp.exp(-x))


def dot(a, b, dims):
    return lax.dot_general(a, b, dims, preferred_element_type=jnp.float32)


def remote(src, dst, send_sem, recv_sem, where):
    return pltpu.make_async_remote_copy(
        src_ref=src,
        dst_ref=dst,
        send_sem=send_sem,
        recv_sem=recv_sem,
        device_id=where,
        device_id_type=pl.DeviceIdType.MESH,
    )


def greet(places):
    barrier = pltpu.get_barrier_semaphore()
    for where in places:
        pl.semaphore_signal(barrier, inc=1, device_id=where, device_id_type=pl.DeviceIdType.MESH)
    pl.semaphore_wait(barrier, len(places))


def scatter_kernel(count, number, peer_of, slot_of, *refs):
    ins, outs = refs[:number], refs[number : 2 * number]
    send_sem, recv_sem, local_sem = refs[2 * number :]
    me = slot_of(lax.axis_index("dap"))
    greet([peer_of(lax.axis_index("dap"), d) for d in range(1, count)])
    keeps = [pltpu.make_async_copy(a.at[me], o.at[me], local_sem.at[i]) for i, (a, o) in enumerate(zip(ins, outs))]
    sends = []
    for d in range(1, count):
        place = peer_of(lax.axis_index("dap"), d)
        target = slot_of(place["dap"])
        for i, (a, o) in enumerate(zip(ins, outs)):
            copy = remote(a.at[target], o.at[me], send_sem.at[i, d], recv_sem.at[i, d], place)
            copy.start()
            sends.append(copy)
    for copy in keeps:
        copy.start()
    for d in range(1, count):
        for i, (a, o) in enumerate(zip(ins, outs)):
            source = lax.rem(me + count - d, count)
            remote(a.at[source], o.at[source], send_sem.at[i, d], recv_sem.at[i, d], peer_of(lax.axis_index("dap"), d)).wait_recv()
    for copy in sends:
        copy.wait_send()
    for copy in keeps:
        copy.wait()


def scatter(arrays, count, peer_of, slot_of, ident, name):
    number = len(arrays)
    return pl.pallas_call(
        functools.partial(scatter_kernel, count, number, peer_of, slot_of),
        in_specs=[pl.BlockSpec(memory_space=pl.ANY)] * number,
        out_specs=[pl.BlockSpec(memory_space=pl.ANY)] * number,
        out_shape=[jax.ShapeDtypeStruct(a.shape, a.dtype) for a in arrays],
        scratch_shapes=[
            pltpu.SemaphoreType.DMA((number, count)),
            pltpu.SemaphoreType.DMA((number, count)),
            pltpu.SemaphoreType.DMA((number,)),
        ],
        compiler_params=pltpu.CompilerParams(collective_id=ident, has_side_effects=True),
        name=name,
    )(*arrays)


def block_kernel(
    ny, nz, share, l_ref, r_ref, lg_ref, rg_ref, fsend, frecv, bsend, brecv, ysend, yrecv, ssend, srecv, local_sem
):
    me = lax.axis_index("dap")
    core = lax.axis_index("branch")
    y, z = me // nz, lax.rem(me, nz)
    up = {"dap": y * nz + lax.rem(z + 1, nz)}
    down = {"dap": y * nz + lax.rem(z + nz - 1, nz)}
    column = [{"dap": lax.rem(y + d, ny) * nz + z} for d in range(1, ny)]
    twin = {"branch": 1 - core}
    greet([up, down] + column + ([twin] if share else []))
    fwd, bwd = nz // 2, nz - 1 - nz // 2

    def slot(which, place):
        return lg_ref.at[which, place] if share else lg_ref.at[place]

    def at(shift):
        return lax.rem(z + nz + shift, nz)

    def ahead(t):
        return remote(l_ref if t == 0 else slot(core, at(-t)), slot(core, at(-t)), fsend.at[t], frecv.at[t], up)

    def back(t):
        return remote(l_ref if t == 0 else slot(core, at(t)), slot(core, at(t)), bsend.at[t], brecv.at[t], down)

    def ahead_in(t):
        return remote(l_ref, slot(core, at(-1 - t)), fsend.at[t], frecv.at[t], up)

    def back_in(t):
        return remote(l_ref, slot(core, at(1 + t)), bsend.at[t], brecv.at[t], down)

    def pass_on(i, shift):
        return remote(l_ref if shift == 0 else slot(core, at(shift)), slot(core, at(shift)), ssend.at[i], srecv.at[i], twin)

    shifts = [0]
    sends = [ahead(0)] + ([back(0)] if bwd else [])
    sends += [remote(r_ref, rg_ref.at[y], ysend.at[d], yrecv.at[d], column[d]) for d in range(ny - 1)]
    if share:
        sends.append(pass_on(0, 0))
    for copy in sends:
        copy.start()
    keeps = [
        pltpu.make_async_copy(l_ref, slot(core, z), local_sem.at[0]),
        pltpu.make_async_copy(r_ref, rg_ref.at[y], local_sem.at[1]),
    ]
    for copy in keeps:
        copy.start()

    def follow(copy):
        copy.start()
        sends.append(copy)

    for t in range(fwd):
        ahead_in(t).wait_recv()
        if t + 1 < fwd:
            follow(ahead(t + 1))
        if share:
            shifts.append(-1 - t)
            follow(pass_on(len(shifts) - 1, -1 - t))
        if t < bwd:
            back_in(t).wait_recv()
            if t + 1 < bwd:
                follow(back(t + 1))
            if share:
                shifts.append(1 + t)
                follow(pass_on(len(shifts) - 1, 1 + t))
    for d in range(ny - 1):
        remote(r_ref, rg_ref.at[lax.rem(y + ny - 1 - d, ny)], ysend.at[d], yrecv.at[d], column[d]).wait_recv()
    if share:
        for i, shift in enumerate(shifts):
            remote(l_ref, slot(1 - core, at(shift)), ssend.at[i], srecv.at[i], twin).wait_recv()
    for copy in sends:
        copy.wait_send()
    for copy in keeps:
        copy.wait()


def gather_blocks(left, right, ny, nz, share, ident, name):
    sems = lambda n: pltpu.SemaphoreType.DMA((n,))
    lead = (2, nz) if share else (nz,)
    return pl.pallas_call(
        functools.partial(block_kernel, ny, nz, share),
        in_specs=[pl.BlockSpec(memory_space=pl.ANY)] * 2,
        out_specs=[pl.BlockSpec(memory_space=pl.ANY)] * 2,
        out_shape=[
            jax.ShapeDtypeStruct(lead + left.shape, left.dtype),
            jax.ShapeDtypeStruct((ny,) + right.shape, right.dtype),
        ],
        scratch_shapes=[sems(nz), sems(nz), sems(nz), sems(nz), sems(ny), sems(ny), sems(nz), sems(nz), sems(2)],
        compiler_params=pltpu.CompilerParams(collective_id=ident, has_side_effects=True),
        name=name,
    )(left, right)


def column_kernel(
    heads, number, send_ref, msend_ref, gain_ref, gain2_ref, w_ref, wo_ref, ws_ref, wt_ref, *refs
):
    extras, (mixed_ref, left_ref, right_ref), both_refs = refs[:number], refs[number : number + 3], refs[number + 3 : 2 * number + 3]
    (
        x_ref, m_ref, w2_ref, wo2_ref, ws2_ref, qkv_ref, gate_ref, gated_ref,
        send_sem, recv_sem, msend_sem, mrecv_sem, keep_sem, tsend_sem, trecv_sem, tkeep_sem,
    ) = refs[2 * number + 3 :]
    res, count, s_loc, width = send_ref.shape
    depth = count * s_loc
    feats = wo2_ref.shape[0] * wo2_ref.shape[1]
    hd = feats // heads
    part = feats // 2
    me = lax.axis_index("dap")
    core = lax.axis_index("branch")
    twin = {"branch": 1 - core}
    barrier = pltpu.get_barrier_semaphore()

    def hello(d, carry):
        pl.semaphore_signal(
            barrier, inc=1, device_id={"dap": lax.rem(me + d, count)}, device_id_type=pl.DeviceIdType.MESH
        )
        return carry

    lax.fori_loop(1, count, hello, 0)
    pl.semaphore_signal(barrier, inc=1, device_id=twin, device_id_type=pl.DeviceIdType.MESH)
    pl.semaphore_wait(barrier, count)

    def give_mask(d, carry):
        peer = lax.rem(me + d, count)
        remote(msend_ref.at[peer], m_ref.at[me], msend_sem.at[0], mrecv_sem.at[0], {"dap": peer}).start()
        return carry

    lax.fori_loop(1, count, give_mask, 0)
    pairs = [(w_ref, w2_ref), (wo_ref, wo2_ref), (ws_ref, ws2_ref)] + list(zip(extras, both_refs))
    swaps = [remote(a, o.at[core], tsend_sem.at[i], trecv_sem.at[i], twin) for i, (a, o) in enumerate(pairs)]
    for copy in swaps:
        copy.start()
    for r in range(res):

        def give(d, carry):
            peer = lax.rem(me + d, count)
            remote(send_ref.at[r, peer], x_ref.at[r, me], send_sem.at[r], recv_sem.at[r], {"dap": peer}).start()
            return carry

        lax.fori_loop(1, count, give, 0)
    keeps = [pltpu.make_async_copy(a, o.at[core], tkeep_sem.at[i]) for i, (a, o) in enumerate(pairs)]
    keeps += [pltpu.make_async_copy(send_ref.at[r, me], x_ref.at[r, me], keep_sem.at[r]) for r in range(res)]
    keeps.append(pltpu.make_async_copy(msend_ref.at[me], m_ref.at[me], keep_sem.at[res]))
    for copy in keeps:
        copy.start()
    for copy in keeps:
        copy.wait()
    for i, (a, o) in enumerate(pairs):
        remote(a, o.at[1 - core], tsend_sem.at[i], trecv_sem.at[i], twin).wait_recv()
    rest = pl.ds(0, count - 1)
    masks = remote(msend_ref.at[rest], m_ref.at[rest], msend_sem.at[0], mrecv_sem.at[0], twin)
    masks.wait_recv()

    m = m_ref[...].reshape(depth, 128)
    rows = lax.broadcasted_iota(jnp.int32, (8, 128), 0)
    lanes = lax.broadcasted_iota(jnp.int32, (8, 128), 1)
    tail = dot((rows == lanes).astype(jnp.bfloat16), m, NT).astype(jnp.bfloat16)
    chans = wt_ref.shape[0]
    left_ref[res * chans :] = tail
    right_ref[res * chans :] = tail
    inv_root = 1.0 / hd**0.5

    @pl.loop(0, res)
    def _(r):
        remote(send_ref.at[r, rest], x_ref.at[r, rest], send_sem.at[r], recv_sem.at[r], twin).wait_recv()
        x = x_ref[r].reshape(depth, width).astype(jnp.float32)
        n = standardize_features(x, gain_ref[...]).astype(jnp.bfloat16)
        for c in range(2):
            proj = dot(w2_ref[c], n, NT)
            for i in range(3):
                qkv_ref[i, c * (heads // 2) : (c + 1) * (heads // 2)] = (
                    proj[i * part : (i + 1) * part].astype(jnp.bfloat16).reshape(heads // 2, hd, depth)
                )
            gate_ref[c * (heads // 2) : (c + 1) * (heads // 2)] = sigmoid(proj[3 * part :]).reshape(heads // 2, hd, depth)
        lane = lax.broadcasted_iota(jnp.int32, (depth, 128), 1)
        mcol = jnp.sum(jnp.where(lane == r, m_ref[...].reshape(depth, 128).astype(jnp.float32), 0.0), axis=1, keepdims=True)
        live = mcol > 0.5

        def one_head(h):
            scores = dot(qkv_ref[1, h], qkv_ref[0, h], TN) * inv_root
            scores = jnp.where(live, scores, -1000000000.0)
            e = jnp.exp(scores - jnp.max(scores, axis=0, keepdims=True))
            total = jnp.sum(e, axis=0, keepdims=True)
            att = jnp.dot(qkv_ref[2, h], e.astype(jnp.bfloat16), preferred_element_type=jnp.float32)
            gated_ref[h] = (att * (1.0 / total) * gate_ref[h]).astype(jnp.bfloat16)

        unroll = 4

        @pl.loop(0, heads // unroll)
        def _(step):
            for u in range(unroll):
                one_head(step * unroll + u)

        gated = gated_ref[...].reshape(feats, depth)
        mixed = (x + dot(gated, wo2_ref[...].reshape(feats, width), TN)).astype(jnp.bfloat16)
        mixed_ref[r] = mixed
        n2 = standardize_features(mixed.astype(jnp.float32), gain2_ref[...]).astype(jnp.bfloat16)
        mrow = dot((lanes == r).astype(jnp.bfloat16), m_ref[...].reshape(depth, 128), NT)[:1]
        where = pl.ds(pl.multiple_of(r * chans, chans), chans)
        left_ref[where] = (dot(ws2_ref[...].reshape(chans, width), n2, NT) * mrow).astype(jnp.bfloat16)
        right_ref[where] = (dot(wt_ref[...], n2, NT) * mrow).astype(jnp.bfloat16)

    for copy in swaps:
        copy.wait_send()
    masks.wait_send()
    for r in range(res):
        remote(send_ref.at[r, rest], x_ref.at[r, rest], send_sem.at[r], recv_sem.at[r], twin).wait_send()


def column_stage(send, msend, gain, gain2, w_t, wo, ws_t, wt_t, extras, heads):
    res, groups, s_loc, width = send.shape
    depth = groups * s_loc
    chans = wt_t.shape[0]
    number = len(extras)
    feats = 2 * wo.shape[0]
    hd = feats // heads
    vmem = pl.BlockSpec(memory_space=pltpu.VMEM)
    hbm = pl.BlockSpec(memory_space=pl.ANY)
    bf16 = jnp.bfloat16
    panel = jax.ShapeDtypeStruct((res * chans + 8, depth), bf16)
    return pl.pallas_call(
        functools.partial(column_kernel, heads, number),
        in_specs=[hbm, hbm] + [vmem] * 6 + [hbm] * number,
        out_specs=[vmem] * 3 + [hbm] * number,
        out_shape=[jax.ShapeDtypeStruct((res, depth, width), bf16), panel, panel]
        + [jax.ShapeDtypeStruct((2,) + a.shape, a.dtype) for a in extras],
        scratch_shapes=[
            pltpu.VMEM(send.shape, bf16),
            pltpu.VMEM(msend.shape, bf16),
            pltpu.VMEM((2,) + w_t.shape, bf16),
            pltpu.VMEM((2,) + wo.shape, bf16),
            pltpu.VMEM((2,) + ws_t.shape, bf16),
            pltpu.VMEM((3, heads, hd, depth), bf16),
            pltpu.VMEM((heads, hd, depth), jnp.float32),
            pltpu.VMEM((heads, hd, depth), bf16),
            pltpu.SemaphoreType.DMA((res,)),
            pltpu.SemaphoreType.DMA((res,)),
            pltpu.SemaphoreType.DMA((1,)),
            pltpu.SemaphoreType.DMA((1,)),
            pltpu.SemaphoreType.DMA((res + 1,)),
            pltpu.SemaphoreType.DMA((3 + number,)),
            pltpu.SemaphoreType.DMA((3 + number,)),
            pltpu.SemaphoreType.DMA((3 + number,)),
        ],
        compiler_params=pltpu.CompilerParams(collective_id=1, has_side_effects=True),
        name="column_attention",
    )(send, msend, gain, gain2, w_t, wo, ws_t, wt_t, *extras)


def outer_kernel(nz, left_ref, right_ref, inv_ref, w_ref, out_ref, prod_ref, made_ref, send_sem, recv_sem, local_sem):
    me = lax.axis_index("dap")
    z = lax.rem(me, nz)
    barrier = pltpu.get_barrier_semaphore()
    peers = [lax.rem(z + d, nz) for d in range(nz)]
    for d in range(1, nz):
        pl.semaphore_signal(
            barrier, inc=1, device_id={"dap": me - z + peers[d]}, device_id_type=pl.DeviceIdType.MESH
        )
    ny = right_ref.shape[0]
    cols, chans = made_ref.shape[1], w_ref.shape[0] // (prod_ref.shape[1] // (2 * inv_ref.shape[0]))
    rows = inv_ref.shape[0]
    wide = 2 * rows
    pairs = prod_ref.shape[1] // wide
    right = jnp.concatenate([right_ref[y, : (cols // ny) * chans] for y in range(ny)], axis=0)
    step = min(512, prod_ref.shape[1])
    for c in range(0, prod_ref.shape[1], step):
        prod_ref[:, c : c + step] = dot(right, left_ref[c : c + step], NT).astype(jnp.bfloat16)
    pl.semaphore_wait(barrier, nz - 1)
    group = 4
    sends = []
    for j in range(cols):
        block = prod_ref[j * chans : (j + 1) * chans]
        block = jnp.concatenate([block[:, p * wide : (p + 1) * wide] for p in range(pairs)], axis=0)
        both = dot(block, w_ref[...], TN)
        width = both.shape[1] // 2
        total = (both[:rows, :width] + both[rows:, width:]) * inv_ref[:, j : j + 1]
        made_ref[:, j] = total.reshape(nz, rows // nz, width).astype(jnp.bfloat16)
        if j % group == group - 1:
            part = pl.ds(j + 1 - group, group)
            for d in range(1, nz):
                copy = remote(
                    made_ref.at[peers[d], part], out_ref.at[z, part], send_sem.at[d], recv_sem.at[d],
                    {"dap": me - z + peers[d]},
                )
                copy.start()
    keep = pltpu.make_async_copy(made_ref.at[z], out_ref.at[z], local_sem.at[0])
    keep.start()
    for d in range(1, nz):
        source = lax.rem(z + nz - d, nz)
        whole = remote(
            made_ref.at[source], out_ref.at[source], send_sem.at[d], recv_sem.at[d], {"dap": me - z + peers[d]}
        )
        whole.wait_recv()
        whole.wait_send()
    keep.wait()


def outer_stage(left, right, inv, w, nz, chans):
    rows, cols = inv.shape
    width = w.shape[1] // 2
    vmem = pl.BlockSpec(memory_space=pltpu.VMEM)
    shape = (nz, cols, rows // nz, width)
    return pl.pallas_call(
        functools.partial(outer_kernel, nz),
        in_specs=[vmem] * 4,
        out_specs=pl.BlockSpec(memory_space=pl.ANY),
        out_shape=jax.ShapeDtypeStruct(shape, jnp.bfloat16),
        scratch_shapes=[
            pltpu.VMEM((cols * chans, left.shape[0]), jnp.bfloat16),
            pltpu.VMEM(shape, jnp.bfloat16),
            pltpu.SemaphoreType.DMA((nz,)),
            pltpu.SemaphoreType.DMA((nz,)),
            pltpu.SemaphoreType.DMA((1,)),
        ],
        compiler_params=pltpu.CompilerParams(collective_id=3, has_side_effects=True),
        name="outer_product",
    )(left, right, inv, w)


def body(
    homolog_features,
    alignment_mask,
    residue_mask,
    pairwise_state,
    vertical_gain_vector,
    fourfold_projection_matrix,
    mixing_projection_matrix,
    product_gain_vector,
    product_source_matrix,
    product_target_matrix,
    outer_output_weight,
    triangle_norm_scale,
    triangle_input_weight,
    triangle_gate_weight,
    hidden_norm_scale,
    triangle_output_weight,
):
    f32, bf16 = jnp.float32, jnp.bfloat16
    groups = lax.axis_size("dap")
    me = lax.axis_index("dap")
    b = lax.axis_index("branch")
    s_loc, residues, width = homolog_features.shape
    res = residues // groups
    half = res // 2
    pair_width = pairwise_state.shape[2]

    def swap(a):
        return lax.ppermute(a, "branch", SWAP)

    def both(own, axis):
        other = swap(own)
        first = b == 0
        return jnp.concatenate([jnp.where(first, own, other), jnp.where(first, other, own)], axis=axis)

    def pick(a, axis, which):
        shape = a.shape
        a = a.reshape(shape[:axis] + (groups, 2, half) + shape[axis + 1 :])
        a = lax.dynamic_index_in_dim(a, which, axis + 1, keepdims=False)
        return a.reshape(shape[:axis] + (groups * half,) + shape[axis + 1 :])

    active = residue_mask.astype(f32)

    heads, hd = 2 * fourfold_projection_matrix.shape[2], fourfold_projection_matrix.shape[3]
    w_t = fourfold_projection_matrix.reshape(width, -1).T
    wo = mixing_projection_matrix.reshape(-1, width)
    chans = product_target_matrix.shape[1]
    hidden = 2 * triangle_input_weight.shape[2]
    extras = [
        outer_output_weight.reshape(-1, pair_width),
        triangle_input_weight.transpose(1, 2, 0),
        triangle_gate_weight.T,
        triangle_output_weight,
        jnp.broadcast_to(hidden_norm_scale[None], (8, hidden // 2)),
    ]

    ny = 4 if groups % 16 == 0 else 2
    nz = groups // ny
    row = lambda i: i - lax.rem(i, nz)
    row_peer = lambda i, d: {"dap": row(i) + lax.rem(lax.rem(i, nz) + d, nz)}
    row_slot = lambda i: lax.rem(i, nz)

    send = pick(homolog_features, 1, b).reshape(s_loc, groups, half, width).transpose(2, 1, 0, 3)
    own_mask = pick((alignment_mask * residue_mask[None, :]).astype(bf16), 1, b)
    own_mask = own_mask.reshape(s_loc, groups, half).transpose(1, 0, 2)
    own_mask = jnp.pad(own_mask, ((0, 0), (0, 0), (0, 128 - half)))
    depth = groups * s_loc
    mixed, left, right, outer_w, tri_in, tri_gate, tri_out, hidden_gain = column_stage(
        send,
        own_mask,
        vertical_gain_vector[None],
        product_gain_vector[None],
        w_t,
        wo,
        product_source_matrix.T,
        product_target_matrix.T,
        extras,
        heads,
    )
    outer_w = outer_w.reshape(chans // 2, 2, chans, pair_width).transpose(0, 2, 1, 3)
    outer_w = outer_w.reshape(chans // 2 * chans, 2 * pair_width)
    tri_in = tri_in.transpose(1, 0, 2, 3).reshape(4 * hidden, pair_width).T
    tri_gate = tri_gate.reshape(pair_width, pair_width).T
    tri_out = tri_out.reshape(hidden, pair_width)
    hidden_gain = hidden_gain[:, 0].reshape(hidden)
    left, right = gather_blocks(left, right, ny, nz, True, 2, "panel_gather")
    homolog_mixed = both(mixed, 0).transpose(1, 0, 2)

    panel_rows = half * chans
    rows_i, cols_j = 2 * nz * half, ny * half
    left_rows = left[:, :, :panel_rows].reshape(2, nz, half, chans, depth)
    left_rows = left_rows.transpose(3, 1, 0, 2, 4).reshape(chans * rows_i, depth)
    counts = dot(
        left[:, :, panel_rows : panel_rows + half].transpose(1, 0, 2, 3).reshape(rows_i, depth),
        right[:, panel_rows : panel_rows + half].reshape(cols_j, depth),
        NT,
    )
    update = outer_stage(left_rows, right, 1.0 / jnp.maximum(counts, 1.0), outer_w, nz, chans)

    def arrange(a):
        a = a.reshape(a.shape[:1] + (ny, nz, 2, half) + a.shape[2:])
        a = lax.dynamic_index_in_dim(a, b, 3, keepdims=False)
        return jnp.swapaxes(a, 1, 2).reshape((a.shape[0], groups * half) + a.shape[4:])

    cols = groups * half
    update = update.transpose(2, 0, 1, 3).reshape(res, cols, pair_width).astype(f32)
    pair_mid = (arrange(pairwise_state).astype(f32) + update).astype(bf16)
    pair_field = pair_mid.astype(f32)
    pair_normed = standardize_features(pair_field, triangle_norm_scale).astype(bf16).reshape(res * cols, pair_width)
    proj = jnp.dot(pair_normed, tri_in, preferred_element_type=f32).reshape(res, cols, 4, hidden)
    row_live = lax.dynamic_slice_in_dim(active, me * res, res, 0)
    live = (row_live[:, None] * arrange(active[None])[0][None, :])[..., None]
    tri_left = (live * sigmoid(proj[:, :, 0]) * proj[:, :, 1]).astype(bf16)
    tri_right = (live * sigmoid(proj[:, :, 2]) * proj[:, :, 3]).astype(bf16)
    gate = sigmoid(jnp.dot(pair_normed, tri_gate, preferred_element_type=f32)).reshape(res, cols, pair_width)

    tri_left, tri_right = gather_blocks(
        tri_left.transpose(2, 0, 1), tri_right.transpose(2, 0, 1), ny, nz, False, 4, "triangle_gather"
    )
    tri_left = tri_left.transpose(1, 0, 2, 3).reshape(hidden, nz * res, cols)
    tri_right = tri_right.reshape(ny, hidden, 2, half, cols).transpose(2, 1, 0, 3, 4).reshape(2, hidden, cols_j, cols)

    def share_of(which):
        chosen = lax.dynamic_index_in_dim(tri_right, which, 0, keepdims=False)
        return jnp.einsum("cik,cjk->cij", tri_left, chosen, preferred_element_type=f32)

    given = swap(share_of(1 - b))
    tri_sum = share_of(b) + given
    mean_val = jnp.mean(tri_sum, axis=0, keepdims=True)
    variance = jnp.mean((tri_sum - mean_val) ** 2, axis=0, keepdims=True)
    tri_scaled = ((tri_sum - mean_val) * lax.rsqrt(variance + eps_norm) * hidden_gain[:, None, None]).astype(bf16)
    projected = dot(tri_scaled, tri_out, TN).astype(bf16)
    (projected,) = scatter(
        [projected.reshape(nz, res, cols_j, pair_width)], nz, row_peer, row_slot, 5, "triangle_exchange"
    )
    projected = projected.transpose(1, 0, 2, 3).reshape(res, cols, pair_width).astype(f32)
    out = (pair_field + gate * projected).astype(bf16)
    z_half = pair_width // 2
    own = lax.dynamic_slice_in_dim(out, b * z_half, z_half, 2)
    other = swap(lax.dynamic_slice_in_dim(out, (1 - b) * z_half, z_half, 2))
    own = own.reshape(res, nz, ny, 1, half, z_half)
    other = other.reshape(res, nz, ny, 1, half, z_half)
    first = b == 0
    out = jnp.concatenate([jnp.where(first, own, other), jnp.where(first, other, own)], axis=3)
    return (homolog_mixed, jnp.swapaxes(out, 1, 2).reshape(res, residues, z_half))


def solution(mesh):
    in_specs = (
        P(("crop", "dap"), None, None),
        P(("crop", "dap"), None),
        P("crop"),
        P(("crop", "dap"), None, None),
        P(),
        P(None, None, "branch", None),
        P("branch", None, None),
        P(),
        P(None, "branch"),
        P(),
        P("branch", None, None),
        P(),
        P(None, None, "branch"),
        P(None, "branch"),
        P("branch"),
        P("branch", None),
    )
    out_specs = (P("crop", "dap", None), P(("crop", "dap"), None, "branch"))
    return jax.shard_map(body, mesh=mesh, in_specs=in_specs, out_specs=out_specs, check_vma=False)
```

```python
import functools

import jax
import jax.numpy as jnp
from jax import lax
from jax.experimental import pallas as pl
from jax.experimental.pallas import tpu as pltpu
from jax.sharding import PartitionSpec as P

eps_norm = 1e-05
SWAP = ((0, 1), (1, 0))
NT = (((1,), (1,)), ((), ()))
TN = (((0,), (0,)), ((), ()))


def standardize_features(field, gain_vec):
    mean_val = jnp.mean(field, axis=-1, keepdims=True)
    variance = jnp.mean((field - mean_val) ** 2, axis=-1, keepdims=True)
    return (field - mean_val) * lax.rsqrt(variance + eps_norm) * gain_vec


def sigmoid(x):
    return 1.0 / (1.0 + jnp.exp(-x))


def dot(a, b, dims):
    return lax.dot_general(a, b, dims, preferred_element_type=jnp.float32)


def remote(src, dst, send_sem, recv_sem, where):
    return pltpu.make_async_remote_copy(
        src_ref=src,
        dst_ref=dst,
        send_sem=send_sem,
        recv_sem=recv_sem,
        device_id=where,
        device_id_type=pl.DeviceIdType.MESH,
    )


def greet(places):
    barrier = pltpu.get_barrier_semaphore()
    for where in places:
        pl.semaphore_signal(barrier, inc=1, device_id=where, device_id_type=pl.DeviceIdType.MESH)
    pl.semaphore_wait(barrier, len(places))


def scatter_kernel(count, number, peer_of, slot_of, *refs):
    ins, outs = refs[:number], refs[number : 2 * number]
    send_sem, recv_sem, local_sem = refs[2 * number :]
    me = slot_of(lax.axis_index("dap"))
    greet([peer_of(lax.axis_index("dap"), d) for d in range(1, count)])
    keeps = [pltpu.make_async_copy(a.at[me], o.at[me], local_sem.at[i]) for i, (a, o) in enumerate(zip(ins, outs))]
    sends = []
    for d in range(1, count):
        place = peer_of(lax.axis_index("dap"), d)
        target = slot_of(place["dap"])
        for i, (a, o) in enumerate(zip(ins, outs)):
            copy = remote(a.at[target], o.at[me], send_sem.at[i, d], recv_sem.at[i, d], place)
            copy.start()
            sends.append(copy)
    for copy in keeps:
        copy.start()
    for d in range(1, count):
        for i, (a, o) in enumerate(zip(ins, outs)):
            source = lax.rem(me + count - d, count)
            remote(a.at[source], o.at[source], send_sem.at[i, d], recv_sem.at[i, d], peer_of(lax.axis_index("dap"), d)).wait_recv()
    for copy in sends:
        copy.wait_send()
    for copy in keeps:
        copy.wait()


def scatter(arrays, count, peer_of, slot_of, ident, name):
    number = len(arrays)
    return pl.pallas_call(
        functools.partial(scatter_kernel, count, number, peer_of, slot_of),
        in_specs=[pl.BlockSpec(memory_space=pl.ANY)] * number,
        out_specs=[pl.BlockSpec(memory_space=pl.ANY)] * number,
        out_shape=[jax.ShapeDtypeStruct(a.shape, a.dtype) for a in arrays],
        scratch_shapes=[
            pltpu.SemaphoreType.DMA((number, count)),
            pltpu.SemaphoreType.DMA((number, count)),
            pltpu.SemaphoreType.DMA((number,)),
        ],
        compiler_params=pltpu.CompilerParams(collective_id=ident, has_side_effects=True),
        name=name,
    )(*arrays)


def block_kernel(
    ny, nz, share, l_ref, r_ref, lg_ref, rg_ref, fsend, frecv, bsend, brecv, ysend, yrecv, ssend, srecv, local_sem
):
    me = lax.axis_index("dap")
    core = lax.axis_index("branch")
    y, z = me // nz, lax.rem(me, nz)
    up = {"dap": y * nz + lax.rem(z + 1, nz)}
    down = {"dap": y * nz + lax.rem(z + nz - 1, nz)}
    column = [{"dap": lax.rem(y + d, ny) * nz + z} for d in range(1, ny)]
    twin = {"branch": 1 - core}
    greet([up, down] + column + ([twin] if share else []))
    long, short = nz // 2, nz - 1 - nz // 2
    fwd, bwd = (long, short), (short, long)
    cut = l_ref.shape[0] // 32 * 16
    spans = (pl.ds(0, cut), pl.ds(cut, l_ref.shape[0] - cut))

    def slot(which, place, q):
        return lg_ref.at[which, place, spans[q]] if share else lg_ref.at[place, spans[q]]

    def at(shift):
        return lax.rem(z + nz + shift, nz)

    def held(shift, q):
        return l_ref.at[spans[q]] if shift == 0 else slot(core, at(shift), q)

    def ahead(t, q):
        return remote(held(-t, q), slot(core, at(-t), q), fsend.at[q, t], frecv.at[q, t], up)

    def back(t, q):
        return remote(held(t, q), slot(core, at(t), q), bsend.at[q, t], brecv.at[q, t], down)

    def ahead_in(t, q):
        return remote(held(0, q), slot(core, at(-1 - t), q), fsend.at[q, t], frecv.at[q, t], up)

    def back_in(t, q):
        return remote(held(0, q), slot(core, at(1 + t), q), bsend.at[q, t], brecv.at[q, t], down)

    def pass_on(i, shift, q):
        return remote(held(shift, q), slot(core, at(shift), q), ssend.at[q, i], srecv.at[q, i], twin)

    shifts = ([], [])
    sends = []

    def follow(copy):
        copy.start()
        sends.append(copy)

    def hand_over(shift, q):
        if share:
            shifts[q].append(shift)
            follow(pass_on(len(shifts[q]) - 1, shift, q))

    for q in range(2):
        if fwd[q]:
            follow(ahead(0, q))
        if bwd[q]:
            follow(back(0, q))
    for d in range(ny - 1):
        follow(remote(r_ref, rg_ref.at[y], ysend.at[d], yrecv.at[d], column[d]))
    for q in range(2):
        hand_over(0, q)
    keeps = [
        pltpu.make_async_copy(l_ref, lg_ref.at[core, z] if share else lg_ref.at[z], local_sem.at[0]),
        pltpu.make_async_copy(r_ref, rg_ref.at[y], local_sem.at[1]),
    ]
    for copy in keeps:
        copy.start()
    for t in range(long):
        for q in range(2):
            if t < fwd[q]:
                ahead_in(t, q).wait_recv()
                if t + 1 < fwd[q]:
                    follow(ahead(t + 1, q))
                hand_over(-1 - t, q)
            if t < bwd[q]:
                back_in(t, q).wait_recv()
                if t + 1 < bwd[q]:
                    follow(back(t + 1, q))
                hand_over(1 + t, q)
    for d in range(ny - 1):
        remote(r_ref, rg_ref.at[lax.rem(y + ny - 1 - d, ny)], ysend.at[d], yrecv.at[d], column[d]).wait_recv()
    for q in range(2):
        for i, shift in enumerate(shifts[q]):
            remote(held(0, q), slot(1 - core, at(shift), q), ssend.at[q, i], srecv.at[q, i], twin).wait_recv()
    for copy in sends:
        copy.wait_send()
    for copy in keeps:
        copy.wait()


def gather_blocks(left, right, ny, nz, share, ident, name):
    sems = lambda n: pltpu.SemaphoreType.DMA((n,))
    pairs = pltpu.SemaphoreType.DMA((2, nz))
    lead = (2, nz) if share else (nz,)
    return pl.pallas_call(
        functools.partial(block_kernel, ny, nz, share),
        in_specs=[pl.BlockSpec(memory_space=pl.ANY)] * 2,
        out_specs=[pl.BlockSpec(memory_space=pl.ANY)] * 2,
        out_shape=[
            jax.ShapeDtypeStruct(lead + left.shape, left.dtype),
            jax.ShapeDtypeStruct((ny,) + right.shape, right.dtype),
        ],
        scratch_shapes=[pairs] * 4 + [sems(ny)] * 2 + [pairs] * 2 + [sems(2)],
        compiler_params=pltpu.CompilerParams(collective_id=ident, has_side_effects=True),
        name=name,
    )(left, right)


def column_kernel(
    heads, number, send_ref, msend_ref, gain_ref, gain2_ref, w_ref, wo_ref, ws_ref, wt_ref, *refs
):
    extras, (mixed_ref, left_ref, right_ref), both_refs = refs[:number], refs[number : number + 3], refs[number + 3 : 2 * number + 3]
    (
        x_ref, m_ref, w2_ref, wo2_ref, ws2_ref, qkv_ref, gate_ref, gated_ref,
        send_sem, recv_sem, msend_sem, mrecv_sem, keep_sem, tsend_sem, trecv_sem, tkeep_sem,
    ) = refs[2 * number + 3 :]
    res, count, s_loc, width = send_ref.shape
    depth = count * s_loc
    feats = wo2_ref.shape[0] * wo2_ref.shape[1]
    hd = feats // heads
    part = feats // 2
    me = lax.axis_index("dap")
    core = lax.axis_index("branch")
    twin = {"branch": 1 - core}
    barrier = pltpu.get_barrier_semaphore()

    def hello(d, carry):
        pl.semaphore_signal(
            barrier, inc=1, device_id={"dap": lax.rem(me + d, count)}, device_id_type=pl.DeviceIdType.MESH
        )
        return carry

    lax.fori_loop(1, count, hello, 0)
    pl.semaphore_signal(barrier, inc=1, device_id=twin, device_id_type=pl.DeviceIdType.MESH)
    pl.semaphore_wait(barrier, count)

    def give_mask(d, carry):
        peer = lax.rem(me + d, count)
        remote(msend_ref.at[peer], m_ref.at[me], msend_sem.at[0], mrecv_sem.at[0], {"dap": peer}).start()
        return carry

    lax.fori_loop(1, count, give_mask, 0)
    pairs = [(w_ref, w2_ref), (wo_ref, wo2_ref), (ws_ref, ws2_ref)] + list(zip(extras, both_refs))
    swaps = [remote(a, o.at[core], tsend_sem.at[i], trecv_sem.at[i], twin) for i, (a, o) in enumerate(pairs)]
    for copy in swaps:
        copy.start()
    for r in range(res):

        def give(d, carry):
            peer = lax.rem(me + d, count)
            remote(send_ref.at[r, peer], x_ref.at[r, me], send_sem.at[r], recv_sem.at[r], {"dap": peer}).start()
            return carry

        lax.fori_loop(1, count, give, 0)
    keeps = [pltpu.make_async_copy(a, o.at[core], tkeep_sem.at[i]) for i, (a, o) in enumerate(pairs)]
    keeps += [pltpu.make_async_copy(send_ref.at[r, me], x_ref.at[r, me], keep_sem.at[r]) for r in range(res)]
    keeps.append(pltpu.make_async_copy(msend_ref.at[me], m_ref.at[me], keep_sem.at[res]))
    for copy in keeps:
        copy.start()
    for copy in keeps:
        copy.wait()
    for i, (a, o) in enumerate(pairs):
        remote(a, o.at[1 - core], tsend_sem.at[i], trecv_sem.at[i], twin).wait_recv()
    rest = pl.ds(0, count - 1)
    masks = remote(msend_ref.at[rest], m_ref.at[rest], msend_sem.at[0], mrecv_sem.at[0], twin)
    masks.wait_recv()

    m = m_ref[...].reshape(depth, 128)
    rows = lax.broadcasted_iota(jnp.int32, (8, 128), 0)
    lanes = lax.broadcasted_iota(jnp.int32, (8, 128), 1)
    tail = dot((rows == lanes).astype(jnp.bfloat16), m, NT).astype(jnp.bfloat16)
    chans = wt_ref.shape[0]
    left_ref[res * chans :] = tail
    right_ref[res * chans :] = tail
    inv_root = 1.0 / hd**0.5

    @pl.loop(0, res)
    def _(r):
        remote(send_ref.at[r, rest], x_ref.at[r, rest], send_sem.at[r], recv_sem.at[r], twin).wait_recv()
        x = x_ref[r].reshape(depth, width).astype(jnp.float32)
        n = standardize_features(x, gain_ref[...]).astype(jnp.bfloat16)
        for c in range(2):
            proj = dot(w2_ref[c], n, NT)
            for i in range(3):
                qkv_ref[i, c * (heads // 2) : (c + 1) * (heads // 2)] = (
                    proj[i * part : (i + 1) * part].astype(jnp.bfloat16).reshape(heads // 2, hd, depth)
                )
            gate_ref[c * (heads // 2) : (c + 1) * (heads // 2)] = sigmoid(proj[3 * part :]).reshape(heads // 2, hd, depth)
        lane = lax.broadcasted_iota(jnp.int32, (depth, 128), 1)
        mcol = jnp.sum(jnp.where(lane == r, m_ref[...].reshape(depth, 128).astype(jnp.float32), 0.0), axis=1, keepdims=True)
        live = mcol > 0.5

        def one_head(h):
            scores = dot(qkv_ref[1, h], qkv_ref[0, h], TN) * inv_root
            scores = jnp.where(live, scores, -1000000000.0)
            e = jnp.exp(scores - jnp.max(scores, axis=0, keepdims=True))
            total = jnp.sum(e, axis=0, keepdims=True)
            att = jnp.dot(qkv_ref[2, h], e.astype(jnp.bfloat16), preferred_element_type=jnp.float32)
            gated_ref[h] = (att * (1.0 / total) * gate_ref[h]).astype(jnp.bfloat16)

        unroll = 4

        @pl.loop(0, heads // unroll)
        def _(step):
            for u in range(unroll):
                one_head(step * unroll + u)

        gated = gated_ref[...].reshape(feats, depth)
        mixed = (x + dot(gated, wo2_ref[...].reshape(feats, width), TN)).astype(jnp.bfloat16)
        mixed_ref[r] = mixed
        n2 = standardize_features(mixed.astype(jnp.float32), gain2_ref[...]).astype(jnp.bfloat16)
        mrow = dot((lanes == r).astype(jnp.bfloat16), m_ref[...].reshape(depth, 128), NT)[:1]
        where = pl.ds(pl.multiple_of(r * chans, chans), chans)
        left_ref[where] = (dot(ws2_ref[...].reshape(chans, width), n2, NT) * mrow).astype(jnp.bfloat16)
        right_ref[where] = (dot(wt_ref[...], n2, NT) * mrow).astype(jnp.bfloat16)

    for copy in swaps:
        copy.wait_send()
    masks.wait_send()
    for r in range(res):
        remote(send_ref.at[r, rest], x_ref.at[r, rest], send_sem.at[r], recv_sem.at[r], twin).wait_send()


def column_stage(send, msend, gain, gain2, w_t, wo, ws_t, wt_t, extras, heads):
    res, groups, s_loc, width = send.shape
    depth = groups * s_loc
    chans = wt_t.shape[0]
    number = len(extras)
    feats = 2 * wo.shape[0]
    hd = feats // heads
    vmem = pl.BlockSpec(memory_space=pltpu.VMEM)
    hbm = pl.BlockSpec(memory_space=pl.ANY)
    bf16 = jnp.bfloat16
    panel = jax.ShapeDtypeStruct((res * chans + 8, depth), bf16)
    return pl.pallas_call(
        functools.partial(column_kernel, heads, number),
        in_specs=[hbm, hbm] + [vmem] * 6 + [hbm] * number,
        out_specs=[vmem] * 3 + [hbm] * number,
        out_shape=[jax.ShapeDtypeStruct((res, depth, width), bf16), panel, panel]
        + [jax.ShapeDtypeStruct((2,) + a.shape, a.dtype) for a in extras],
        scratch_shapes=[
            pltpu.VMEM(send.shape, bf16),
            pltpu.VMEM(msend.shape, bf16),
            pltpu.VMEM((2,) + w_t.shape, bf16),
            pltpu.VMEM((2,) + wo.shape, bf16),
            pltpu.VMEM((2,) + ws_t.shape, bf16),
            pltpu.VMEM((3, heads, hd, depth), bf16),
            pltpu.VMEM((heads, hd, depth), jnp.float32),
            pltpu.VMEM((heads, hd, depth), bf16),
            pltpu.SemaphoreType.DMA((res,)),
            pltpu.SemaphoreType.DMA((res,)),
            pltpu.SemaphoreType.DMA((1,)),
            pltpu.SemaphoreType.DMA((1,)),
            pltpu.SemaphoreType.DMA((res + 1,)),
            pltpu.SemaphoreType.DMA((3 + number,)),
            pltpu.SemaphoreType.DMA((3 + number,)),
            pltpu.SemaphoreType.DMA((3 + number,)),
        ],
        compiler_params=pltpu.CompilerParams(collective_id=1, has_side_effects=True),
        name="column_attention",
    )(send, msend, gain, gain2, w_t, wo, ws_t, wt_t, *extras)


def outer_kernel(nz, left_ref, right_ref, inv_ref, w_ref, out_ref, prod_ref, made_ref, send_sem, recv_sem, local_sem):
    me = lax.axis_index("dap")
    z = lax.rem(me, nz)
    barrier = pltpu.get_barrier_semaphore()
    peers = [lax.rem(z + d, nz) for d in range(nz)]
    for d in range(1, nz):
        pl.semaphore_signal(
            barrier, inc=1, device_id={"dap": me - z + peers[d]}, device_id_type=pl.DeviceIdType.MESH
        )
    ny = right_ref.shape[0]
    cols, chans = made_ref.shape[1], w_ref.shape[0] // (prod_ref.shape[1] // (2 * inv_ref.shape[0]))
    rows = inv_ref.shape[0]
    wide = 2 * rows
    pairs = prod_ref.shape[1] // wide
    right = jnp.concatenate([right_ref[y, : (cols // ny) * chans] for y in range(ny)], axis=0)
    step = min(512, prod_ref.shape[1])
    for c in range(0, prod_ref.shape[1], step):
        prod_ref[:, c : c + step] = dot(right, left_ref[c : c + step], NT).astype(jnp.bfloat16)
    pl.semaphore_wait(barrier, nz - 1)
    group = 4
    sends = []
    for j in range(cols):
        block = prod_ref[j * chans : (j + 1) * chans]
        block = jnp.concatenate([block[:, p * wide : (p + 1) * wide] for p in range(pairs)], axis=0)
        both = dot(block, w_ref[...], TN)
        width = both.shape[1] // 2
        total = (both[:rows, :width] + both[rows:, width:]) * inv_ref[:, j : j + 1]
        made_ref[:, j] = total.reshape(nz, rows // nz, width).astype(jnp.bfloat16)
        if j % group == group - 1:
            part = pl.ds(j + 1 - group, group)
            for d in range(1, nz):
                copy = remote(
                    made_ref.at[peers[d], part], out_ref.at[z, part], send_sem.at[d], recv_sem.at[d],
                    {"dap": me - z + peers[d]},
                )
                copy.start()
    keep = pltpu.make_async_copy(made_ref.at[z], out_ref.at[z], local_sem.at[0])
    keep.start()
    for d in range(1, nz):
        source = lax.rem(z + nz - d, nz)
        whole = remote(
            made_ref.at[source], out_ref.at[source], send_sem.at[d], recv_sem.at[d], {"dap": me - z + peers[d]}
        )
        whole.wait_recv()
        whole.wait_send()
    keep.wait()


def outer_stage(left, right, inv, w, nz, chans):
    rows, cols = inv.shape
    width = w.shape[1] // 2
    vmem = pl.BlockSpec(memory_space=pltpu.VMEM)
    shape = (nz, cols, rows // nz, width)
    return pl.pallas_call(
        functools.partial(outer_kernel, nz),
        in_specs=[vmem] * 4,
        out_specs=pl.BlockSpec(memory_space=pl.ANY),
        out_shape=jax.ShapeDtypeStruct(shape, jnp.bfloat16),
        scratch_shapes=[
            pltpu.VMEM((cols * chans, left.shape[0]), jnp.bfloat16),
            pltpu.VMEM(shape, jnp.bfloat16),
            pltpu.SemaphoreType.DMA((nz,)),
            pltpu.SemaphoreType.DMA((nz,)),
            pltpu.SemaphoreType.DMA((1,)),
        ],
        compiler_params=pltpu.CompilerParams(collective_id=3, has_side_effects=True),
        name="outer_product",
    )(left, right, inv, w)


def body(
    homolog_features,
    alignment_mask,
    residue_mask,
    pairwise_state,
    vertical_gain_vector,
    fourfold_projection_matrix,
    mixing_projection_matrix,
    product_gain_vector,
    product_source_matrix,
    product_target_matrix,
    outer_output_weight,
    triangle_norm_scale,
    triangle_input_weight,
    triangle_gate_weight,
    hidden_norm_scale,
    triangle_output_weight,
):
    f32, bf16 = jnp.float32, jnp.bfloat16
    groups = lax.axis_size("dap")
    me = lax.axis_index("dap")
    b = lax.axis_index("branch")
    s_loc, residues, width = homolog_features.shape
    res = residues // groups
    half = res // 2
    pair_width = pairwise_state.shape[2]

    def swap(a):
        return lax.ppermute(a, "branch", SWAP)

    def both(own, axis):
        other = swap(own)
        first = b == 0
        return jnp.concatenate([jnp.where(first, own, other), jnp.where(first, other, own)], axis=axis)

    def pick(a, axis, which):
        shape = a.shape
        a = a.reshape(shape[:axis] + (groups, 2, half) + shape[axis + 1 :])
        a = lax.dynamic_index_in_dim(a, which, axis + 1, keepdims=False)
        return a.reshape(shape[:axis] + (groups * half,) + shape[axis + 1 :])

    active = residue_mask.astype(f32)

    heads, hd = 2 * fourfold_projection_matrix.shape[2], fourfold_projection_matrix.shape[3]
    w_t = fourfold_projection_matrix.reshape(width, -1).T
    wo = mixing_projection_matrix.reshape(-1, width)
    chans = product_target_matrix.shape[1]
    hidden = 2 * triangle_input_weight.shape[2]
    extras = [
        outer_output_weight.reshape(-1, pair_width),
        triangle_input_weight.transpose(1, 2, 0),
        triangle_gate_weight.T,
        triangle_output_weight,
        jnp.broadcast_to(hidden_norm_scale[None], (8, hidden // 2)),
    ]

    ny = 4 if groups % 16 == 0 else 2
    nz = groups // ny
    row = lambda i: i - lax.rem(i, nz)
    row_peer = lambda i, d: {"dap": row(i) + lax.rem(lax.rem(i, nz) + d, nz)}
    row_slot = lambda i: lax.rem(i, nz)

    send = pick(homolog_features, 1, b).reshape(s_loc, groups, half, width).transpose(2, 1, 0, 3)
    own_mask = pick((alignment_mask * residue_mask[None, :]).astype(bf16), 1, b)
    own_mask = own_mask.reshape(s_loc, groups, half).transpose(1, 0, 2)
    own_mask = jnp.pad(own_mask, ((0, 0), (0, 0), (0, 128 - half)))
    depth = groups * s_loc
    mixed, left, right, outer_w, tri_in, tri_gate, tri_out, hidden_gain = column_stage(
        send,
        own_mask,
        vertical_gain_vector[None],
        product_gain_vector[None],
        w_t,
        wo,
        product_source_matrix.T,
        product_target_matrix.T,
        extras,
        heads,
    )
    outer_w = outer_w.reshape(chans // 2, 2, chans, pair_width).transpose(0, 2, 1, 3)
    outer_w = outer_w.reshape(chans // 2 * chans, 2 * pair_width)
    tri_in = tri_in.transpose(1, 0, 2, 3).reshape(4 * hidden, pair_width).T
    tri_gate = tri_gate.reshape(pair_width, pair_width).T
    tri_out = tri_out.reshape(hidden, pair_width)
    hidden_gain = hidden_gain[:, 0].reshape(hidden)
    left, right = gather_blocks(left, right, ny, nz, True, 2, "panel_gather")
    homolog_mixed = both(mixed, 0).transpose(1, 0, 2)

    panel_rows = half * chans
    rows_i, cols_j = 2 * nz * half, ny * half
    left_rows = left[:, :, :panel_rows].reshape(2, nz, half, chans, depth)
    left_rows = left_rows.transpose(3, 1, 0, 2, 4).reshape(chans * rows_i, depth)
    counts = dot(
        left[:, :, panel_rows : panel_rows + half].transpose(1, 0, 2, 3).reshape(rows_i, depth),
        right[:, panel_rows : panel_rows + half].reshape(cols_j, depth),
        NT,
    )
    update = outer_stage(left_rows, right, 1.0 / jnp.maximum(counts, 1.0), outer_w, nz, chans)

    def arrange(a):
        a = a.reshape(a.shape[:1] + (ny, nz, 2, half) + a.shape[2:])
        a = lax.dynamic_index_in_dim(a, b, 3, keepdims=False)
        return jnp.swapaxes(a, 1, 2).reshape((a.shape[0], groups * half) + a.shape[4:])

    cols = groups * half
    update = update.transpose(2, 0, 1, 3).reshape(res, cols, pair_width).astype(f32)
    pair_mid = (arrange(pairwise_state).astype(f32) + update).astype(bf16)
    pair_field = pair_mid.astype(f32)
    pair_normed = standardize_features(pair_field, triangle_norm_scale).astype(bf16).reshape(res * cols, pair_width)
    proj = jnp.dot(pair_normed, tri_in, preferred_element_type=f32).reshape(res, cols, 4, hidden)
    row_live = lax.dynamic_slice_in_dim(active, me * res, res, 0)
    live = (row_live[:, None] * arrange(active[None])[0][None, :])[..., None]
    tri_left = (live * sigmoid(proj[:, :, 0]) * proj[:, :, 1]).astype(bf16)
    tri_right = (live * sigmoid(proj[:, :, 2]) * proj[:, :, 3]).astype(bf16)
    gate = sigmoid(jnp.dot(pair_normed, tri_gate, preferred_element_type=f32)).reshape(res, cols, pair_width)

    tri_left, tri_right = gather_blocks(
        tri_left.transpose(2, 0, 1), tri_right.transpose(2, 0, 1), ny, nz, False, 4, "triangle_gather"
    )
    tri_left = tri_left.transpose(1, 0, 2, 3).reshape(hidden, nz * res, cols)
    tri_right = tri_right.reshape(ny, hidden, 2, half, cols).transpose(2, 1, 0, 3, 4).reshape(2, hidden, cols_j, cols)

    def share_of(which):
        chosen = lax.dynamic_index_in_dim(tri_right, which, 0, keepdims=False)
        return jnp.einsum("cik,cjk->cij", tri_left, chosen, preferred_element_type=f32)

    given = swap(share_of(1 - b))
    tri_sum = share_of(b) + given
    mean_val = jnp.mean(tri_sum, axis=0, keepdims=True)
    variance = jnp.mean((tri_sum - mean_val) ** 2, axis=0, keepdims=True)
    tri_scaled = ((tri_sum - mean_val) * lax.rsqrt(variance + eps_norm) * hidden_gain[:, None, None]).astype(bf16)
    projected = dot(tri_scaled, tri_out, TN).astype(bf16)
    (projected,) = scatter(
        [projected.reshape(nz, res, cols_j, pair_width)], nz, row_peer, row_slot, 5, "triangle_exchange"
    )
    projected = projected.transpose(1, 0, 2, 3).reshape(res, cols, pair_width).astype(f32)
    out = (pair_field + gate * projected).astype(bf16)
    z_half = pair_width // 2
    own = lax.dynamic_slice_in_dim(out, b * z_half, z_half, 2)
    other = swap(lax.dynamic_slice_in_dim(out, (1 - b) * z_half, z_half, 2))
    own = own.reshape(res, nz, ny, 1, half, z_half)
    other = other.reshape(res, nz, ny, 1, half, z_half)
    first = b == 0
    out = jnp.concatenate([jnp.where(first, own, other), jnp.where(first, other, own)], axis=3)
    return (homolog_mixed, jnp.swapaxes(out, 1, 2).reshape(res, residues, z_half))


def solution(mesh):
    in_specs = (
        P(("crop", "dap"), None, None),
        P(("crop", "dap"), None),
        P("crop"),
        P(("crop", "dap"), None, None),
        P(),
        P(None, None, "branch", None),
        P("branch", None, None),
        P(),
        P(None, "branch"),
        P(),
        P("branch", None, None),
        P(),
        P(None, None, "branch"),
        P(None, "branch"),
        P("branch"),
        P("branch", None),
    )
    out_specs = (P("crop", "dap", None), P(("crop", "dap"), None, "branch"))
    return jax.shard_map(body, mesh=mesh, in_specs=in_specs, out_specs=out_specs, check_vma=False)
```
